32 devices in a mesh: dp: 8 (over y, x, core), tensor: 4 (over z).
Axes of the slice: x: 2, y: 2, z: 4, core: 2. Of those that a mesh axis runs over, the one named last changes fastest.
Arguments:
- residual: bfloat16 [4096, 4096], P(('dp', 'tensor')), may hold values from -3 to 3
- queries: bfloat16 [4096, 4096], P(('dp', 'tensor')), may hold values from -8 to 8
- rotated_key_states: bfloat16 [4096, 512], P(('dp', 'tensor')), may hold values from -8 to 8
- plain_value_states: bfloat16 [4096, 512], P(('dp', 'tensor')), may hold values from -24 to 24
- out_weight: bfloat16 [4096, 4096], P('tensor'), may hold values from -0.09375 to 0.09375
- norm_gain: bfloat16 [4096], replicated, may hold values from 0.099609375 to 1.8984375
- expert_ids: int32 [4096, 8], P(('dp', 'tensor')), may hold values from 0 to 31, all different within a row; in each aligned block of 128 rows (0 to 127, 128 to 255, ...) at most 36 rows name the same one
- gate_scales: float32 [4096, 8], P(('dp', 'tensor')), may hold values from 0.03 to 0.3
- w_gate: bfloat16 [32, 4096, 768], P(('dp', 'tensor')), may hold values from -0.09375 to 0.09375
- w_up: bfloat16 [32, 4096, 768], P(('dp', 'tensor')), may hold values from -0.09375 to 0.09375
- w_down: bfloat16 [32, 768, 4096], P(('dp', 'tensor')), may hold values from -0.21875 to 0.21875
Outputs:
- layer_out: bfloat16 [4096, 4096], P(('dp', 'tensor'))
The draws below stay inside these ranges and needn't reach their ends.
Inputs may be any that keep to these rules, and one draw needn't show every extreme that they name: `expert_ids`: each row names 8 different experts; among the rows of one device (aligned blocks of 128 rows) no expert is named more than 36 times.
All inputs are finite; a program needn't handle non-finite values.
Results may differ from the reference program's by a relative error of at most 0.012.
Values may be sent and summed in bfloat16 or wider, within the bound.
No kernel may reach another device: no remote copies, remote signals or barrier semaphores. Data moves between devices by JAX's collectives and lax.ppermute only.
A program may use at most 192 MiB of HBM per device.

```python
import math
import jax
import jax.numpy as jnp
import numpy as np
from jax import lax

D = 4096
QUERY_HEADS = 32
KEY_VALUE_HEADS = 4
HEAD_SIZE = 128
FW = 768
TOPK = 8
TOK_DEV = 128
SEQUENCE_LENGTH = 512
TOKEN_COUNT = 4096
E = 32
CAP = 36
N_TENSOR = 4


def draw_queries(key, part):
    sampled_values = jax.random.truncated_normal(jax.random.fold_in(key, 1), -6.0, 6.0, (TOKEN_COUNT, QUERY_HEADS * HEAD_SIZE), jnp.float32)
    return sampled_values.astype(jnp.bfloat16)


def draw_rotated_key_states(key, part):
    sampled_values = jax.random.truncated_normal(jax.random.fold_in(key, 2), -6.0, 6.0, (TOKEN_COUNT, KEY_VALUE_HEADS * HEAD_SIZE), jnp.float32)
    return sampled_values.astype(jnp.bfloat16)


def block_scale(own_key, dims, shards, smallest, top_value):
    gain, own = 1.0, jax.random.fold_in(own_key, 6)
    for dim, parts in shards:
        steps = jnp.exp(jax.random.uniform(jax.random.fold_in(own, dim), (parts,), jnp.float32, smallest / len(shards), top_value / len(shards)))
        gain = gain * jnp.repeat(steps, dims[dim] // parts).reshape([-1 if axis == dim else 1 for axis in range(len(dims))])
    return gain


def assign_block(key, own, number, rows, amount, top, reach, skew):
    sequence = jax.random.permutation(key, amount)
    packed, usual = portions_of(amount, rows * top, reach, skew, True), portions_of(amount, rows * top, reach, skew, False)
    places = jnp.arange(amount)

    def named(lengths, rotation):
        used = int((lengths > 0).sum())
        fixed = max(1, used // 4)
        moved = fixed + (places - fixed + rotation * (used - fixed)) % max(1, amount - fixed)
        return jnp.zeros((amount,), jnp.int32).at[sequence[jnp.where(places < fixed, places, moved)]].set(jnp.asarray(lengths, jnp.int32))

    lengths = jnp.where(number % 4 == 0, named(packed, number // 4), named(usual, number - number // 4 - 1))
    mixed = jax.random.permutation(jax.random.fold_in(own, 3), amount)
    source_of, taker = mixed[0:amount // 2 * 2:2], mixed[1:amount // 2 * 2:2]
    slack = jnp.minimum(lengths[source_of] - 1, reach - lengths[taker]) // 2
    slack = jnp.where((source_of == sequence[0]) | (taker == sequence[0]) | (lengths[taker] == 0), 0, jnp.maximum(slack, 0))
    moved = jax.random.randint(jax.random.fold_in(own, 4), (amount // 2,), 0, 1 << 20) % (slack + 1)
    lengths = lengths.at[source_of].add(-moved).at[taker].add(moved)
    items = jnp.searchsorted(jnp.cumsum(lengths), jnp.arange(rows * top), side="right").astype(jnp.int32)
    table = items.reshape(top, rows).T
    table = table[jax.random.permutation(jax.random.fold_in(own, 1), rows)]
    rotation = jax.random.randint(jax.random.fold_in(own, 2), (rows, 1), 0, top)
    return jnp.take_along_axis(table, (jnp.arange(top)[None, :] + rotation) % top, axis=1)


def portions_of(count, total, most, slope, full):
    loads = [(1 << 20) // math.isqrt(rank ** slope) + 1 for rank in range(1, count + 1)]
    largest = most if full else min(most, max(-(-total // count), total * loads[0] // sum(loads)))
    least = 1 if total - largest >= count - 1 else 0
    counts, surplus = [largest] + [least] * (count - 1), total - largest - least * (count - 1)
    while surplus > 0:
        movable = [i for i in range(1, count) if counts[i] < largest] or [i for i in range(1, count) if counts[i] < most]
        pool, budget = sum([loads[i] for i in movable]), surplus
        for i in movable:
            addition = min(most - counts[i], max(1, budget * loads[i] // pool), surplus)
            counts[i] = counts[i] + addition
            surplus = surplus - addition
    return np.array(counts)


def noise(key, extent, spread, reach, cuts=(), kind=jnp.bfloat16):
    level = block_scale(key, extent, cuts, -0.22, 0.18) if cuts else 1.0
    array = jax.random.normal(key, extent, jnp.float32) * spread * level
    return jnp.minimum(jnp.maximum(array, -reach), reach).astype(kind)


def setup_inputs(seed: int = 0) -> dict:
    streams_of = jax.random.split(jax.random.key(seed), 12)
    residual = noise(streams_of[0], (TOKEN_COUNT, D), 0.5, 3.0, ((0, 32),))
    queries = draw_queries(jax.random.fold_in(streams_of[11], 71), 0)
    rotated_key_states = draw_rotated_key_states(jax.random.fold_in(streams_of[11], 71), 0)
    plain_value_states = noise(streams_of[3], (TOKEN_COUNT, KEY_VALUE_HEADS * HEAD_SIZE), 4.0, 24.0, ((0, 32),))
    out_weight = noise(streams_of[4], (QUERY_HEADS * HEAD_SIZE, D), (QUERY_HEADS * HEAD_SIZE) ** -0.5, 0.09375, ((0, 4),))
    norm_gain = jnp.clip(1.0 + 0.18 * jax.random.normal(streams_of[5], (D,), jnp.float32), 0.099609375, 1.8984375).astype(jnp.bfloat16)
    expert_ids_keys = jax.random.split(jax.random.fold_in(streams_of[6], 1), TOKEN_COUNT // TOK_DEV)
    expert_ids_turns = jax.random.permutation(jax.random.fold_in(streams_of[6], 3), TOKEN_COUNT // TOK_DEV)
    expert_ids = jax.vmap(lambda own, number: assign_block(jax.random.fold_in(streams_of[6], 2), own, number, TOK_DEV, E, TOPK, CAP, 2))(expert_ids_keys, expert_ids_turns).reshape((TOKEN_COUNT, TOPK))
    gate_scales = jnp.clip(jnp.exp(math.log(0.3) - 2.3025852 * jax.random.uniform(streams_of[7], (TOKEN_COUNT, TOPK), jnp.float32) ** block_scale(streams_of[7], (TOKEN_COUNT, TOPK), ((0, 32),), -0.2, 0.2)), 0.03, 0.3)
    w_gate = noise(streams_of[8], (E, D, FW), D ** -0.5, 0.09375, ((0, 32),))
    w_up = noise(streams_of[9], (E, D, FW), D ** -0.5, 0.09375, ((0, 32),))
    w_down = noise(streams_of[10], (E, FW, D), FW ** -0.5, 0.21875, ((0, 32),))
    return {"residual": residual, "queries": queries, "rotated_key_states": rotated_key_states, "plain_value_states": plain_value_states, "out_weight": out_weight, "norm_gain": norm_gain, "expert_ids": expert_ids, "gate_scales": gate_scales, "w_gate": w_gate, "w_up": w_up, "w_down": w_down}


def attend_single_sequence(operands):
    query_row_set, key_row_set, value_row_set = operands
    query_group = QUERY_HEADS // KEY_VALUE_HEADS
    query_complete = query_row_set.astype(jnp.float32).reshape(SEQUENCE_LENGTH, KEY_VALUE_HEADS, query_group, HEAD_SIZE)
    key_complete = key_row_set.astype(jnp.float32).reshape(SEQUENCE_LENGTH, KEY_VALUE_HEADS, HEAD_SIZE)
    value_complete = value_row_set.astype(jnp.float32).reshape(SEQUENCE_LENGTH, KEY_VALUE_HEADS, HEAD_SIZE)
    scores = jnp.einsum('tkgd,nkd->kgtn', query_complete, key_complete) / math.sqrt(HEAD_SIZE)
    places = jnp.arange(SEQUENCE_LENGTH, dtype=jnp.int32)
    visible = places[None, :] <= places[:, None]
    scores = jnp.where(visible, scores, -1e+30)
    highest = lax.optimization_barrier(jnp.max(scores, axis=-1, keepdims=True))
    expons = jnp.where(visible, jnp.exp(scores - highest), 0.0)
    totals = lax.optimization_barrier(jnp.sum(expons, axis=-1))
    rounded = lax.optimization_barrier(expons.astype(jnp.bfloat16)).astype(jnp.float32)
    blended = jnp.einsum('kgtn,nkd->kgtd', rounded, value_complete) / totals[..., None]
    return jnp.transpose(blended, (2, 0, 1, 3)).reshape(SEQUENCE_LENGTH, QUERY_HEADS * HEAD_SIZE).astype(jnp.bfloat16)

def reference(residual, queries, rotated_key_states, plain_value_states, out_weight, norm_gain, expert_ids, gate_scales, w_gate, w_up, w_down):
    sequence_list = TOKEN_COUNT // SEQUENCE_LENGTH
    attended_rows = lax.map(attend_single_sequence, (queries.reshape(sequence_list, SEQUENCE_LENGTH, QUERY_HEADS * HEAD_SIZE), rotated_key_states.reshape(sequence_list, SEQUENCE_LENGTH, KEY_VALUE_HEADS * HEAD_SIZE), plain_value_states.reshape(sequence_list, SEQUENCE_LENGTH, KEY_VALUE_HEADS * HEAD_SIZE)))
    attended_rows = attended_rows.reshape(TOKEN_COUNT, QUERY_HEADS * HEAD_SIZE)
    width_block = QUERY_HEADS * HEAD_SIZE // N_TENSOR
    projected = jnp.zeros((TOKEN_COUNT, D), jnp.float32)
    for block_index in range(N_TENSOR):
        lower_col = block_index * width_block
        partial_sum = jnp.dot(attended_rows[:, lower_col:lower_col + width_block], out_weight[lower_col:lower_col + width_block], preferred_element_type=jnp.float32)
        projected = projected + lax.optimization_barrier(partial_sum.astype(jnp.bfloat16)).astype(jnp.float32)
    hidden_state = residual.astype(jnp.float32) + projected
    inverse_rms = lax.rsqrt(lax.optimization_barrier(jnp.mean(hidden_state * hidden_state, axis=-1, keepdims=True)) + 1e-06)
    normed = (hidden_state * inverse_rms * norm_gain.astype(jnp.float32)).astype(jnp.bfloat16)
    device_count = TOKEN_COUNT // TOK_DEV
    pair_count = TOK_DEV * TOPK
    chosen = expert_ids.reshape(device_count, pair_count)
    onehot = (chosen[:, :, None] == jnp.arange(E, dtype=jnp.int32)[None, None, :]).astype(jnp.int32)
    earlier = jnp.cumsum(onehot, axis=1) - onehot
    slots = lax.optimization_barrier(jnp.sum(earlier * onehot, axis=-1)).astype(jnp.int32)
    sources = jnp.broadcast_to(jnp.arange(device_count, dtype=jnp.int32)[:, None], (device_count, pair_count))
    labels = jnp.broadcast_to(jnp.arange(1, pair_count + 1, dtype=jnp.int32)[None, :], (device_count, pair_count))
    owner = jnp.zeros((E, device_count, CAP), jnp.int32).at[chosen, sources, slots].set(labels)
    gates_flat = gate_scales.astype(jnp.float32).reshape(-1)

    def expert_step(moe_sum, operands):
        owned, gate_mat, up_mat, down_mat = operands
        valid = owned > 0
        base_pair = jnp.arange(device_count, dtype=jnp.int32)[:, None] * pair_count
        pair_index = jnp.where(valid, base_pair + owned - 1, 0).reshape(-1).astype(jnp.int32)
        valid_flat = valid.reshape(-1)
        token_row = (pair_index // TOPK).astype(jnp.int32)
        rows_in = jnp.where(valid_flat[:, None], normed[token_row], jnp.zeros((), jnp.bfloat16))
        gate_part = jnp.dot(rows_in, gate_mat, preferred_element_type=jnp.float32)
        up_part = jnp.dot(rows_in, up_mat, preferred_element_type=jnp.float32)
        activated = (jax.nn.silu(gate_part) * up_part).astype(jnp.bfloat16)
        produced = jnp.dot(activated, down_mat, preferred_element_type=jnp.float32).astype(jnp.bfloat16)
        produced_wide = lax.optimization_barrier(produced).astype(jnp.float32)
        weight = jnp.where(valid_flat, gates_flat[pair_index], 0.0)
        moe_sum = moe_sum.at[token_row].add(weight[:, None] * produced_wide)
        return (moe_sum, None)
    moe_sum, _ = lax.scan(expert_step, jnp.zeros((TOKEN_COUNT, D), jnp.float32), (owner, w_gate, w_up, w_down))
    return (hidden_state + moe_sum).astype(jnp.bfloat16)
```

```python
import functools
import math

import jax
import jax.numpy as jnp
from jax import lax
from jax.experimental import pallas as pl
from jax.experimental.pallas import tpu as pltpu
from jax.sharding import PartitionSpec as P

D = 4096
QUERY_HEADS = 32
KEY_VALUE_HEADS = 4
HEAD_SIZE = 128
TOPK = 8


def attend_kernel(q_ref, k_ref, v_ref, o_ref, *, block):
    scaling = 1.0 / math.sqrt(HEAD_SIZE)
    total = q_ref.shape[0]
    rows = lax.broadcasted_iota(jnp.int32, (block, block), 0)
    cols = lax.broadcasted_iota(jnp.int32, (block, block), 1)
    for first in range(0, total, block):
        seen = first + block
        scores = (
            lax.dot_general(
                q_ref[first:seen, :],
                k_ref[:seen, :],
                (((1,), (1,)), ((), ())),
                preferred_element_type=jnp.float32,
            )
            * scaling
        )
        diagonal = jnp.where(cols <= rows, scores[:, first:], -1e30)
        if first:
            scores = jnp.concatenate([scores[:, :first], diagonal], axis=1)
        else:
            scores = diagonal
        peak = jnp.max(scores, axis=-1, keepdims=True)
        expons = jnp.exp(scores - peak)
        totals = jnp.sum(expons, axis=-1, keepdims=True)
        mixed = jnp.dot(
            expons.astype(jnp.bfloat16), v_ref[:seen, :], preferred_element_type=jnp.float32
        )
        o_ref[first:seen, :] = (mixed / totals).astype(jnp.bfloat16)


def attend(slab, heads):
    positions = slab.shape[0]
    return pl.pallas_call(
        functools.partial(attend_kernel, block=128),
        grid=(heads,),
        in_specs=[
            pl.BlockSpec((positions, HEAD_SIZE), lambda h: (0, h)),
            pl.BlockSpec((positions, HEAD_SIZE), lambda h: (0, heads)),
            pl.BlockSpec((positions, HEAD_SIZE), lambda h: (0, heads + 1)),
        ],
        out_specs=pl.BlockSpec((positions, HEAD_SIZE), lambda h: (0, h)),
        out_shape=jax.ShapeDtypeStruct((positions, heads * HEAD_SIZE), jnp.bfloat16),
    )(slab, slab, slab)


def run_expert(rows_in, gate_mat, up_mat, down_mat):
    gate_part = jnp.dot(rows_in, gate_mat, preferred_element_type=jnp.float32)
    up_part = jnp.dot(rows_in, up_mat, preferred_element_type=jnp.float32)
    activated = (jax.nn.silu(gate_part) * up_part).astype(jnp.bfloat16)
    return jnp.dot(activated, down_mat, preferred_element_type=jnp.float32).astype(jnp.bfloat16)


def swap(value, axis, distance, size):
    return lax.ppermute(value, axis, [(i, i ^ distance) for i in range(size)])


def exchange(rows, size):
    parted = rows.reshape(size, rows.shape[0] // size, rows.shape[1])
    parted = lax.all_to_all(parted, "dp", split_axis=0, concat_axis=0, tiled=True)
    return parted.reshape(rows.shape)


def after(*values):
    return lax.optimization_barrier(values)


def selection(ids, gates, experts, slot_count):
    match = (ids[:, :, None] == experts[None, None, :]).astype(jnp.float32)
    chosen = jnp.sum(match, axis=1)
    weight = jnp.sum(match * gates[:, :, None], axis=1)
    rows = ids.shape[0]
    order = jnp.arange(rows, dtype=jnp.int32)
    earlier = (order[:, None] > order[None, :]).astype(jnp.bfloat16)
    ranks = jnp.dot(earlier, chosen.astype(jnp.bfloat16), preferred_element_type=jnp.float32)
    slots = jnp.where(chosen > 0, ranks.astype(jnp.int32), -1)
    places = jnp.arange(slot_count, dtype=jnp.int32)
    hit = slots[:, :, None] == places[None, None, :]
    count = experts.shape[0] * slot_count
    pick = hit.astype(jnp.bfloat16).reshape(rows, count)
    blend = jnp.where(hit, weight[:, :, None], 0.0).reshape(rows, count)
    blend_high = blend.astype(jnp.bfloat16)
    blend_low = (blend - blend_high.astype(jnp.float32)).astype(jnp.bfloat16)
    return pick, blend_high, blend_low


def per_device(
    residual,
    queries,
    rotated_key_states,
    plain_value_states,
    out_weight,
    norm_gain,
    expert_ids,
    gate_scales,
    w_gate,
    w_up,
    w_down,
):
    row_count = residual.shape[0]
    tensor_size = lax.axis_size("tensor")
    dp_size = lax.axis_size("dp")
    my_tensor = lax.axis_index("tensor")
    my_dp = lax.axis_index("dp")
    heads = QUERY_HEADS // tensor_size
    shares = tensor_size // KEY_VALUE_HEADS

    routing = jnp.concatenate([expert_ids.astype(jnp.float32), gate_scales], axis=1)

    def by_head(states):
        states = states.reshape(row_count, KEY_VALUE_HEADS, HEAD_SIZE)
        return jnp.repeat(states, shares, axis=1) if shares > 1 else states

    slabs = jnp.concatenate(
        [
            queries.reshape(row_count, tensor_size, heads * HEAD_SIZE),
            by_head(rotated_key_states),
            by_head(plain_value_states),
        ],
        axis=2,
    )
    slab = lax.all_to_all(slabs, "tensor", split_axis=1, concat_axis=0, tiled=True)
    slab = slab.reshape(tensor_size * row_count, (heads + 2) * HEAD_SIZE)
    attended = attend(slab, heads)
    projected = lax.psum_scatter(
        jnp.dot(attended, out_weight, preferred_element_type=jnp.float32).astype(jnp.bfloat16),
        "tensor",
        scatter_dimension=0,
        tiled=True,
    ).astype(jnp.float32)
    hidden_state = residual.astype(jnp.float32) + projected
    inverse_rms = lax.rsqrt(jnp.mean(hidden_state * hidden_state, axis=-1, keepdims=True) + 1e-06)
    normed = (hidden_state * inverse_rms * norm_gain.astype(jnp.float32)).astype(jnp.bfloat16)

    capacity = 9 * row_count // (dp_size * tensor_size)
    experts = jnp.arange(dp_size, dtype=jnp.int32) * tensor_size + my_tensor

    slot_count = -(-capacity // 8) * 8

    def dispatch(block, plan):
        outgoing = lax.dot_general(
            plan[0], block, (((0,), (0,)), ((), ())), preferred_element_type=jnp.float32
        ).astype(jnp.bfloat16)
        return outgoing

    def combine(returned, plan):
        return jnp.dot(plan[1], returned, preferred_element_type=jnp.float32) + jnp.dot(
            plan[2], returned, preferred_element_type=jnp.float32
        )

    def expert(arrived):
        return run_expert(arrived, w_gate[0], w_up[0], w_down[0])

    def plan_for(routing):
        return selection(routing[:, :TOPK].astype(jnp.int32), routing[:, TOPK:], experts, slot_count)

    def short(value):
        return value.astype(jnp.bfloat16)

    def long(value):
        return value.astype(jnp.float32)

    if tensor_size == 4:
        pairs = [(0, 1), (1, 0), (2, 3), (3, 2)]
        middle = [(1, 2), (2, 1)]
        outward = [(1, 0), (2, 3)]
        inward = [(0, 1), (3, 2)]

        def send(value, moves):
            return lax.ppermute(value, "tensor", moves)

        def spread(block):
            near = send(block, pairs)
            inner_two = send(block, middle)
            outer_two = send(inner_two, outward)
            inner_three = send(near, middle)
            outer_three = send(inner_three, outward)
            return near, inner_two, outer_two, inner_three, outer_three

        r_near, r_in2, r_out2, r_in3, r_out3 = spread(routing)
        plans = [plan_for(r) for r in (routing, r_near, r_in2 + r_out2, r_in3 + r_out3)]

        out0 = dispatch(normed, plans[0])
        arr0 = exchange(out0, dp_size)
        source, _ = after(normed, out0)
        near = send(source, pairs)
        inner_two = send(source, middle)
        near, inner_two = after(near, inner_two)
        outer_two = send(inner_two, outward)
        inner_three = send(near, middle)
        out1 = dispatch(near, plans[1])
        arr1 = exchange(out1, dp_size)
        arr0, _ = after(arr0, out1)
        pro0 = expert(arr0)
        outer_two, inner_three, _ = after(outer_two, inner_three, pro0)
        outer_three = send(inner_three, outward)
        out2 = dispatch(inner_two + outer_two, plans[2])
        arr2 = exchange(out2, dp_size)
        arr1, _ = after(arr1, out2)
        pro1 = expert(arr1)
        outer_three, _ = after(outer_three, pro1)
        out3 = dispatch(inner_three + outer_three, plans[3])
        arr3 = exchange(out3, dp_size)
        arr2, _ = after(arr2, out3)
        pro2 = expert(arr2)
        arr3, _ = after(arr3, pro2)
        pro3 = expert(arr3)
        ret3 = exchange(pro3, dp_size)
        pro2, ret3 = after(pro2, ret3)
        ret2 = exchange(pro2, dp_size)
        part3 = short(combine(ret3, plans[3]))
        far3 = send(part3, inward)
        pro1, ret2, far3 = after(pro1, ret2, far3)
        ret1 = exchange(pro1, dp_size)
        part2 = short(combine(ret2, plans[2]))
        far2 = send(part2, inward)
        mid3 = send(short(long(part3) + long(far3)), middle)
        pro0, ret1, mid3, far2 = after(pro0, ret1, mid3, far2)
        ret0 = exchange(pro0, dp_size)
        part1 = short(combine(ret1, plans[1]) + long(mid3))
        last1 = send(part1, pairs)
        last2 = send(short(long(part2) + long(far2)), middle)
        moe_sum = combine(ret0, plans[0]) + long(last1) + long(last2)
    else:
        blocks = {0: normed}
        moe_sum = None
        for step in range(tensor_size):
            if step:
                low = step & -step
                blocks[step] = swap(blocks[step ^ low], "tensor", low, tensor_size)
            plan = plan_for(swap(routing, "tensor", step, tensor_size) if step else routing)
            arrived = exchange(dispatch(blocks[step], plan), dp_size)
            part = combine(exchange(expert(arrived), dp_size), plan)
            if step:
                part = long(swap(short(part), "tensor", step, tensor_size))
            moe_sum = part if moe_sum is None else moe_sum + part
    return (hidden_state + moe_sum).astype(jnp.bfloat16)


def solution(mesh):
    placed = (
        P(("dp", "tensor"), None),
        P(("dp", "tensor"), None),
        P(("dp", "tensor"), None),
        P(("dp", "tensor"), None),
        P("tensor", None),
        P(),
        P(("dp", "tensor"), None),
        P(("dp", "tensor"), None),
        P(("dp", "tensor"), None, None),
        P(("dp", "tensor"), None, None),
        P(("dp", "tensor"), None, None),
    )
    return jax.shard_map(
        per_device, mesh=mesh, in_specs=placed, out_specs=P(("dp", "tensor"), None), check_vma=False
    )
```

```python
import functools
import math

import jax
import jax.numpy as jnp
from jax import lax
from jax.experimental import pallas as pl
from jax.experimental.pallas import tpu as pltpu
from jax.sharding import PartitionSpec as P

D = 4096
QUERY_HEADS = 32
KEY_VALUE_HEADS = 4
HEAD_SIZE = 128
TOPK = 8


def attend_kernel(q_ref, k_ref, v_ref, o_ref, *, block):
    scaling = 1.0 / math.sqrt(HEAD_SIZE)
    total = q_ref.shape[0]
    rows = lax.broadcasted_iota(jnp.int32, (block, block), 0)
    cols = lax.broadcasted_iota(jnp.int32, (block, block), 1)
    for first in range(0, total, block):
        seen = first + block
        scores = (
            lax.dot_general(
                q_ref[first:seen, :],
                k_ref[:seen, :],
                (((1,), (1,)), ((), ())),
                preferred_element_type=jnp.float32,
            )
            * scaling
        )
        diagonal = jnp.where(cols <= rows, scores[:, first:], -1e30)
        if first:
            scores = jnp.concatenate([scores[:, :first], diagonal], axis=1)
        else:
            scores = diagonal
        peak = jnp.max(scores, axis=-1, keepdims=True)
        expons = jnp.exp(scores - peak)
        totals = jnp.sum(expons, axis=-1, keepdims=True)
        mixed = jnp.dot(
            expons.astype(jnp.bfloat16), v_ref[:seen, :], preferred_element_type=jnp.float32
        )
        o_ref[first:seen, :] = (mixed / totals).astype(jnp.bfloat16)


def attend(slab, heads):
    positions = slab.shape[0]
    return pl.pallas_call(
        functools.partial(attend_kernel, block=128),
        grid=(heads,),
        in_specs=[
            pl.BlockSpec((positions, HEAD_SIZE), lambda h: (0, h)),
            pl.BlockSpec((positions, HEAD_SIZE), lambda h: (0, heads)),
            pl.BlockSpec((positions, HEAD_SIZE), lambda h: (0, heads + 1)),
        ],
        out_specs=pl.BlockSpec((positions, HEAD_SIZE), lambda h: (0, h)),
        out_shape=jax.ShapeDtypeStruct((positions, heads * HEAD_SIZE), jnp.bfloat16),
    )(slab, slab, slab)


def slot_plan(capacity):
    whole = capacity // 8 * 8
    if capacity - whole > 4:
        whole += 8
    return whole, max(capacity - whole, 0)


def per_source(refs, sources, stride):
    if len(refs) == 1:
        return [(refs[0], source * stride) for source in range(sources)]
    return [(ref, 0) for ref in refs]


def expert_kernel(*refs, arrays_in, arrays_out, sources, whole, rest, tile):
    rows_refs, refs = refs[:arrays_in], refs[arrays_in:]
    gate_ref, up_ref, down_ref = refs[:3]
    out_refs, refs = refs[3 : 3 + arrays_out], refs[3 + arrays_out :]
    full_ref, act_ref, gates, ups, downs, sems = refs
    width, units = gate_ref.shape
    half = width // 2
    tiles = units // tile
    pieces = []
    for index in range(tiles):
        window = slice(index * tile, (index + 1) * tile)
        pieces.append((gate_ref.at[:, window], gates.at[index]))
        pieces.append((up_ref.at[:, window], ups.at[index]))
    for side in range(2):
        pieces.append((down_ref.at[:, side * half : (side + 1) * half], downs.at[side]))
    copies = [
        pltpu.make_async_copy(source, target, sems.at[index])
        for index, (source, target) in enumerate(pieces)
    ]
    for copy in copies:
        copy.start()
    stride = 2 * whole + (8 if rest else 0)
    count = sources * whole
    taken = per_source(rows_refs, sources, stride)
    for source, (ref, base) in enumerate(taken):
        for side in range(2):
            first = base + side * whole
            full_ref[source * whole : (source + 1) * whole, side * half : (side + 1) * half] = ref[
                first : first + whole, :
            ]
    if rest:
        last = [ref[base + 2 * whole : base + stride, :].astype(jnp.float32) for ref, base in taken]
        last = jnp.concatenate(last, axis=0)
        full_ref[count:, :half] = last.astype(jnp.bfloat16)
        full_ref[count:, half:] = pltpu.roll(last, last.shape[0] - 4, 0).astype(jnp.bfloat16)
    for index in range(tiles):
        copies[2 * index].wait()
        gate_part = jnp.dot(full_ref[...], gates[index], preferred_element_type=jnp.float32)
        copies[2 * index + 1].wait()
        up_part = jnp.dot(full_ref[...], ups[index], preferred_element_type=jnp.float32)
        act_ref[:, index * tile : (index + 1) * tile] = (
            gate_part / (1.0 + jnp.exp(-gate_part)) * up_part
        ).astype(jnp.bfloat16)
    copies[2 * tiles].wait()
    copies[2 * tiles + 1].wait()
    given = per_source(out_refs, sources, stride)
    for first in range(0, half, 1024):
        window = slice(first, first + 1024)
        kept = None
        for side in range(2):
            produced = jnp.dot(
                act_ref[...],
                downs[side, :, window],
                preferred_element_type=jnp.float32,
            )
            rounded = produced[:count].astype(jnp.bfloat16)
            for source, (ref, base) in enumerate(given):
                top = base + side * whole
                ref[top : top + whole, window] = rounded[source * whole : (source + 1) * whole]
            if rest and side == 0:
                kept = produced[count:]
            elif rest:
                moved = pltpu.roll(produced[count:], 4, 0)
                low = lax.broadcasted_iota(jnp.int32, kept.shape, 0) % 8 < 4
                merged = jnp.where(low, kept, moved).astype(jnp.bfloat16)
                for source, (ref, base) in enumerate(given):
                    ref[base + 2 * whole : base + stride, window] = merged[source * 8 : (source + 1) * 8]


def run_expert(arrived, weights, sources, whole, rest, arrays_out, tile=256):
    width, units = weights[0].shape
    padded = sources * (whole + (8 if rest else 0))
    stride = 2 * whole + (8 if rest else 0)
    out_shape = jax.ShapeDtypeStruct((sources * stride // arrays_out, width // 2), jnp.bfloat16)
    inside = pl.BlockSpec(memory_space=pltpu.VMEM)
    return pl.pallas_call(
        functools.partial(
            expert_kernel,
            arrays_in=len(arrived),
            arrays_out=arrays_out,
            sources=sources,
            whole=whole,
            rest=rest,
            tile=tile,
        ),
        in_specs=[inside] * len(arrived) + [pl.BlockSpec(memory_space=pl.ANY)] * 3,
        out_specs=[inside] * arrays_out,
        out_shape=[out_shape] * arrays_out,
        scratch_shapes=[
            pltpu.VMEM((padded, width), jnp.bfloat16),
            pltpu.VMEM((padded, units), jnp.bfloat16),
            pltpu.VMEM((units // tile, width, tile), jnp.bfloat16),
            pltpu.VMEM((units // tile, width, tile), jnp.bfloat16),
            pltpu.VMEM((2, units, width // 2), jnp.bfloat16),
            pltpu.SemaphoreType.DMA((2 * (units // tile) + 2,)),
        ],
        compiler_params=pltpu.CompilerParams(vmem_limit_bytes=48 * 1024 * 1024),
        cost_estimate=pl.CostEstimate(
            flops=6 * padded * width * units, transcendentals=padded * units, bytes_accessed=40_000_000
        ),
    )(*arrived, *weights)


def gather_kernel(pick_ref, *refs, block_count):
    block_refs, out_refs = refs[:block_count], refs[block_count:]
    block = block_refs[0][...]
    for ref in block_refs[1:]:
        block = block + ref[...]
    step = pick_ref.shape[0] // len(out_refs)
    for index, ref in enumerate(out_refs):
        ref[...] = jnp.dot(
            pick_ref[index * step : (index + 1) * step, :], block, preferred_element_type=jnp.float32
        ).astype(jnp.bfloat16)


def gather_rows(pick, blocks, arrays_out):
    out_shape = jax.ShapeDtypeStruct((pick.shape[0] // arrays_out, blocks[0].shape[1]), jnp.bfloat16)
    inside = pl.BlockSpec(memory_space=pltpu.VMEM)
    return pl.pallas_call(
        functools.partial(gather_kernel, block_count=len(blocks)),
        in_specs=[inside] * (1 + len(blocks)),
        out_specs=[inside] * arrays_out,
        out_shape=[out_shape] * arrays_out,
        cost_estimate=pl.CostEstimate(
            flops=2 * pick.size * blocks[0].shape[1], transcendentals=0, bytes_accessed=4_000_000
        ),
    )(pick, *blocks)


def combine_kernel(blend_ref, rows_ref, *out_refs):
    rows = out_refs[0].shape[0]
    for first in range(0, rows_ref.shape[1], 512):
        window = slice(first, first + 512)
        for index, ref in enumerate(out_refs):
            ref[:, window] = jnp.dot(
                blend_ref[index * rows : (index + 1) * rows, :],
                rows_ref[:, window],
                preferred_element_type=jnp.float32,
            ).astype(ref.dtype)


def combine_rows(blend, returned, kind, arrays_out=1):
    out_shape = jax.ShapeDtypeStruct((blend.shape[0] // arrays_out, returned.shape[1]), kind)
    inside = pl.BlockSpec(memory_space=pltpu.VMEM)
    return pl.pallas_call(
        combine_kernel,
        in_specs=[inside] * 2,
        out_specs=[inside] * arrays_out,
        out_shape=[out_shape] * arrays_out,
        cost_estimate=pl.CostEstimate(
            flops=2 * blend.size * out_shape.shape[1], transcendentals=0, bytes_accessed=4_000_000
        ),
    )(blend, returned)


def swap(value, axis, distance, size):
    return lax.ppermute(value, axis, [(i, i ^ distance) for i in range(size)])


def exchange(rows, size):
    if len(rows) > 1:
        return [swap(part, "dp", k, size) if k else part for k, part in enumerate(rows)]
    (rows,) = rows
    parted = rows.reshape(size, rows.shape[0] // size, rows.shape[1])
    parted = lax.all_to_all(parted, "dp", split_axis=0, concat_axis=0, tiled=True)
    return [parted.reshape(rows.shape)]


def after(*values):
    return lax.optimization_barrier(values)


def selection(ids, gates, experts, whole, rest):
    match = (ids[:, :, None] == experts[None, None, :]).astype(jnp.float32)
    chosen = jnp.sum(match, axis=1)
    weight = jnp.sum(match * gates[:, :, None], axis=1)
    rows = ids.shape[0]
    order = jnp.arange(rows, dtype=jnp.int32)
    earlier = (order[:, None] > order[None, :]).astype(jnp.bfloat16)
    ranks = jnp.dot(earlier, chosen.astype(jnp.bfloat16), preferred_element_type=jnp.float32)
    slot_of = jnp.where(chosen > 0, ranks.astype(jnp.int32), -1)
    stride = 2 * whole + (8 if rest else 0)
    column = jnp.arange(experts.shape[0] * stride, dtype=jnp.int32)
    owner, inner = column // stride, column % stride
    ending = inner - 2 * whole
    side = jnp.where(ending < 0, inner // max(whole, 1), ending // 4)
    place = jnp.where(ending < 0, inner % max(whole, 1), whole + ending % 4)
    place = jnp.where(place < whole + rest, place, -2)
    count = column.shape[0]
    expand = owner[None, :] == jnp.arange(experts.shape[0], dtype=jnp.int32)[:, None]
    wide_slot = jnp.sum(jnp.where(expand[None], slot_of[:, :, None], 0), axis=1)
    wide_weight = jnp.sum(jnp.where(expand[None], weight[:, :, None], 0.0), axis=1)
    sides = jnp.arange(2, dtype=jnp.int32)
    hit = (wide_slot == place[None, :])[None] & (side[None, None, :] == sides[:, None, None])
    blend = jnp.where(hit, wide_weight[None], 0.0).reshape(2 * rows, count).astype(jnp.bfloat16)
    pick = hit.reshape(2 * rows, count).astype(jnp.bfloat16).T
    return pick, blend


def per_device(
    residual,
    queries,
    rotated_key_states,
    plain_value_states,
    out_weight,
    norm_gain,
    expert_ids,
    gate_scales,
    w_gate,
    w_up,
    w_down,
):
    row_count = residual.shape[0]
    tensor_size = lax.axis_size("tensor")
    dp_size = lax.axis_size("dp")
    my_tensor = lax.axis_index("tensor")
    my_dp = lax.axis_index("dp")
    heads = QUERY_HEADS // tensor_size
    shares = tensor_size // KEY_VALUE_HEADS

    routing = jnp.concatenate([expert_ids.astype(jnp.float32), gate_scales], axis=1)

    def by_head(states):
        states = states.reshape(row_count, KEY_VALUE_HEADS, HEAD_SIZE)
        return jnp.repeat(states, shares, axis=1) if shares > 1 else states

    slabs = jnp.concatenate(
        [
            queries.reshape(row_count, tensor_size, heads * HEAD_SIZE),
            by_head(rotated_key_states),
            by_head(plain_value_states),
        ],
        axis=2,
    )
    slab = lax.all_to_all(slabs, "tensor", split_axis=1, concat_axis=0, tiled=True)
    slab = slab.reshape(tensor_size * row_count, (heads + 2) * HEAD_SIZE)
    attended = attend(slab, heads)
    projected = lax.psum_scatter(
        jnp.dot(attended, out_weight, preferred_element_type=jnp.float32).astype(jnp.bfloat16),
        "tensor",
        scatter_dimension=0,
        tiled=True,
    ).astype(jnp.float32)
    hidden_state = residual.astype(jnp.float32) + projected
    inverse_rms = lax.rsqrt(jnp.mean(hidden_state * hidden_state, axis=-1, keepdims=True) + 1e-06)
    normed = (hidden_state * inverse_rms * norm_gain.astype(jnp.float32)).astype(jnp.bfloat16)
    normed = jnp.concatenate([normed[:, : D // 2], normed[:, D // 2 :]], axis=0)

    capacity = 9 * row_count // (dp_size * tensor_size)
    peers = jnp.arange(dp_size, dtype=jnp.int32)
    whole, rest = slot_plan(capacity)

    weights = (w_gate[0], w_up[0], w_down[0])

    def plan_for(routing, arrays):
        owners = peers if arrays == 1 else my_dp ^ peers
        return selection(
            routing[:, :TOPK].astype(jnp.int32),
            routing[:, TOPK:],
            owners * tensor_size + my_tensor,
            whole,
            rest,
        )

    def expert(arrived):
        return run_expert(arrived, weights, dp_size, whole, rest, len(arrived))

    def short(value):
        return value.astype(jnp.bfloat16)

    def long(value):
        return value.astype(jnp.float32)

    if tensor_size == 4:
        pairs = [(0, 1), (1, 0), (2, 3), (3, 2)]
        middle = [(1, 2), (2, 1)]
        outward = [(1, 0), (2, 3)]
        inward = [(0, 1), (3, 2)]
        ends = [(0, 3), (3, 0)]
        skips = [(1, 3), (2, 0)]

        def send(value, moves):
            return lax.ppermute(value, "tensor", moves)

        def spread(block):
            near = send(block, pairs)
            inner_two = send(block, middle)
            outer_two = send(inner_two, outward)
            inner_three = send(near, middle)
            outer_three = send(inner_three, outward)
            return near, inner_two, outer_two, inner_three, outer_three

        r_near, r_in2, r_out2, r_in3, r_out3 = spread(routing)
        arrays = (1, 1, 1, 1)
        plans = [
            plan_for(r, n)
            for r, n in zip((routing, r_near, r_in2 + r_out2, r_in3 + r_out3), arrays)
        ]

        normed, *flat = after(normed, *[part for plan in plans for part in plan])
        plans = list(zip(flat[::2], flat[1::2]))

        def dispatch(blocks, chunk):
            return gather_rows(plans[chunk][0], blocks, arrays[chunk])

        def combine(returned, chunk, kind=jnp.bfloat16, arrays_out=1):
            return list(combine_rows(plans[chunk][1], returned[0], kind, arrays_out))

        near = send(normed, pairs)
        inner_two = send(normed, middle)
        out0 = dispatch([normed], 0)
        arr0 = exchange(out0, dp_size)
        near, inner_two, _ = after(near, inner_two, out0)
        outer_two = send(inner_two, outward)
        inner_three = send(near, middle)
        out1 = dispatch([near], 1)
        arr1 = exchange(out1, dp_size)
        arr0, _ = after(arr0, out1)
        pro0 = expert(arr0)
        outer_two, inner_three, _ = after(outer_two, inner_three, pro0)
        outer_three = send(inner_three, outward)
        out2 = dispatch([inner_two, outer_two], 2)
        arr2 = exchange(out2, dp_size)
        arr1, _ = after(arr1, out2)
        pro1 = expert(arr1)
        outer_three, _ = after(outer_three, pro1)
        out3 = dispatch([inner_three, outer_three], 3)
        arr3 = exchange(out3, dp_size)
        arr2, pro1, _ = after(arr2, pro1, out3)
        pro2 = expert(arr2)
        arr3, pro2 = after(arr3, pro2)
        ret2 = exchange(pro2, dp_size)
        pro3 = expert(arr3)
        ret2, pro3 = after(ret2, pro3)
        ret3 = exchange(pro3, dp_size)
        part2 = combine(ret2, 2, arrays_out=2)
        far2 = [send(part2[side], inward) for side in range(2)]
        pro1, ret3, far2[0], far2[1] = after(pro1, ret3, *far2)
        ret1 = exchange(pro1, dp_size)
        part3 = combine(ret3, 3, arrays_out=2)
        far3 = [send(part3[side], inward) for side in range(2)]
        part2[0], part2[1], _ = after(*part2, part3[0])
        last2 = [send(short(long(part2[side]) + long(far2[side])), middle) for side in range(2)]
        pro0, ret1, far3[0], far3[1], last2[0], last2[1] = after(pro0, ret1, *far3, *last2)
        ret0 = exchange(pro0, dp_size)
        mid3 = [send(short(long(part3[0]) + long(far3[0])), middle), None]
        mid3[0], far3[1] = after(mid3[0], far3[1])
        mid3[1] = send(short(long(part3[1]) + long(far3[1])), middle)
        part1 = combine(ret1, 1, jnp.float32, arrays_out=2)
        last1 = [send(short(part1[side] + long(mid3[side])), pairs) for side in range(2)]
        home = combine(ret0, 0, jnp.float32, arrays_out=2)
        moe_sum = jnp.concatenate(
            [home[side] + long(last1[side]) + long(last2[side]) for side in range(2)], axis=0
        )
    else:
        blocks = {0: normed}
        moe_sum = 0.0
        for step in range(tensor_size):
            if step:
                low = step & -step
                blocks[step] = swap(blocks[step ^ low], "tensor", low, tensor_size)
            plan = plan_for(swap(routing, "tensor", step, tensor_size) if step else routing, 1)
            arrived = exchange(gather_rows(plan[0], [blocks[step]], 1), dp_size)
            (blended,) = combine_rows(plan[1], exchange(expert(arrived), dp_size)[0], jnp.float32)
            if step:
                blended = long(swap(short(blended), "tensor", step, tensor_size))
            moe_sum = moe_sum + blended
    moe_sum = jnp.concatenate([moe_sum[:row_count], moe_sum[row_count:]], axis=1)
    return (hidden_state + moe_sum).astype(jnp.bfloat16)


def solution(mesh):
    placed = (
        P(("dp", "tensor"), None),
        P(("dp", "tensor"), None),
        P(("dp", "tensor"), None),
        P(("dp", "tensor"), None),
        P("tensor", None),
        P(),
        P(("dp", "tensor"), None),
        P(("dp", "tensor"), None),
        P(("dp", "tensor"), None, None),
        P(("dp", "tensor"), None, None),
        P(("dp", "tensor"), None, None),
    )
    return jax.shard_map(
        per_device, mesh=mesh, in_specs=placed, out_specs=P(("dp", "tensor"), None), check_vma=False
    )
```

```python
import functools
import math

import jax
import jax.numpy as jnp
from jax import lax
from jax.experimental import pallas as pl
from jax.experimental.pallas import tpu as pltpu
from jax.sharding import PartitionSpec as P

D = 4096
QUERY_HEADS = 32
KEY_VALUE_HEADS = 4
HEAD_SIZE = 128
TOPK = 8


def attend_kernel(
    q_ref, k_ref, v_ref, weight_ref, o_ref, attended_ref, held_ref, sem, *, block, attend_steps
):
    step = pl.program_id(0)
    scaling = 1.0 / math.sqrt(HEAD_SIZE)
    total, lanes = q_ref.shape
    heads = lanes // HEAD_SIZE
    fetch = pltpu.make_async_copy(weight_ref, held_ref, sem)

    @pl.when(step == 0)
    def _():
        fetch.start()

    @pl.when(step < attend_steps)
    def _():
        rows = lax.broadcasted_iota(jnp.int32, (block, block), 0)
        cols = lax.broadcasted_iota(jnp.int32, (block, block), 1)
        for first in range(0, total, block):
            seen = first + block
            mixes = []
            for head in range(heads):
                scores = (
                    lax.dot_general(
                        q_ref[first:seen, head * HEAD_SIZE : (head + 1) * HEAD_SIZE],
                        k_ref[:seen, :],
                        (((1,), (1,)), ((), ())),
                        preferred_element_type=jnp.float32,
                    )
                    * scaling
                )
                diagonal = jnp.where(cols <= rows, scores[:, first:], -1e30)
                if first:
                    scores = jnp.concatenate([scores[:, :first], diagonal], axis=1)
                else:
                    scores = diagonal
                peak = jnp.max(scores, axis=-1, keepdims=True)
                expons = jnp.exp(scores - peak)
                totals = jnp.sum(expons, axis=-1, keepdims=True)
                mixed = jnp.dot(
                    expons.astype(jnp.bfloat16), v_ref[:seen, :], preferred_element_type=jnp.float32
                )
                mixes.append((mixed / totals).astype(jnp.bfloat16))
            start = pl.multiple_of(step * lanes, lanes)
            attended_ref[first:seen, pl.ds(start, lanes)] = jnp.concatenate(mixes, axis=1)

    @pl.when(step == attend_steps)
    def _():
        fetch.wait()

    @pl.when(step >= attend_steps)
    def _():
        tile = o_ref.shape[1]
        start = pl.multiple_of((step - attend_steps) * tile, tile)
        o_ref[...] = jnp.dot(
            attended_ref[...], held_ref[:, pl.ds(start, tile)], preferred_element_type=jnp.float32
        ).astype(jnp.bfloat16)


def attend_and_project(slab, out_weight, heads, tile=512):
    positions = slab.shape[0]
    width = out_weight.shape[1]
    out_weight = pltpu.with_memory_space_constraint(out_weight, pltpu.HBM)
    group = 2 if heads % 2 == 0 else 1
    attend_steps = heads // group
    last = attend_steps - 1
    return pl.pallas_call(
        functools.partial(attend_kernel, block=128, attend_steps=attend_steps),
        grid=(attend_steps + width // tile,),
        in_specs=[
            pl.BlockSpec((positions, group * HEAD_SIZE), lambda i: (0, jnp.minimum(i, last))),
            pl.BlockSpec((positions, HEAD_SIZE), lambda i: (0, heads)),
            pl.BlockSpec((positions, HEAD_SIZE), lambda i: (0, heads + 1)),
            pl.BlockSpec(memory_space=pl.ANY),
        ],
        out_specs=pl.BlockSpec((positions, tile), lambda i: (0, jnp.maximum(i - attend_steps, 0))),
        out_shape=pltpu.HBM((positions, width), jnp.bfloat16),
        scratch_shapes=[
            pltpu.VMEM((positions, heads * HEAD_SIZE), jnp.bfloat16),
            pltpu.VMEM(out_weight.shape, jnp.bfloat16),
            pltpu.SemaphoreType.DMA,
        ],
        compiler_params=pltpu.CompilerParams(vmem_limit_bytes=40 * 1024 * 1024),
    )(slab, slab, slab, out_weight)


def slot_plan(capacity):
    whole = capacity // 8 * 8
    if capacity - whole > 4:
        whole += 8
    return whole, max(capacity - whole, 0)


def per_source(refs, sources, stride):
    if len(refs) == 1:
        return [(refs[0], source * stride) for source in range(sources)]
    return [(ref, 0) for ref in refs]


def expert_kernel(*refs, arrays_in, arrays_out, sources, whole, rest, tile):
    rows_refs, refs = refs[:arrays_in], refs[arrays_in:]
    gate_ref, up_ref, down_ref = refs[:3]
    out_refs, refs = refs[3 : 3 + arrays_out], refs[3 + arrays_out :]
    full_ref, act_ref, gates, ups, downs, sems = refs
    width, units = gate_ref.shape
    half = width // 2
    tiles = units // tile
    pieces = []
    for index in range(tiles):
        window = slice(index * tile, (index + 1) * tile)
        pieces.append((gate_ref.at[:, window], gates.at[index]))
        pieces.append((up_ref.at[:, window], ups.at[index]))
    for side in range(2):
        pieces.append((down_ref.at[:, side * half : (side + 1) * half], downs.at[side]))
    copies = [
        pltpu.make_async_copy(source, target, sems.at[index])
        for index, (source, target) in enumerate(pieces)
    ]
    for copy in copies:
        copy.start()
    stride = 2 * whole + (8 if rest else 0)
    count = sources * whole
    taken = per_source(rows_refs, sources, stride)
    for source, (ref, base) in enumerate(taken):
        for side in range(2):
            first = base + side * whole
            full_ref[source * whole : (source + 1) * whole, side * half : (side + 1) * half] = ref[
                first : first + whole, :
            ]
    if rest:
        last = [ref[base + 2 * whole : base + stride, :].astype(jnp.float32) for ref, base in taken]
        last = jnp.concatenate(last, axis=0)
        full_ref[count:, :half] = last.astype(jnp.bfloat16)
        full_ref[count:, half:] = pltpu.roll(last, last.shape[0] - 4, 0).astype(jnp.bfloat16)
    def gated(index, carry):
        window = pl.ds(pl.multiple_of(index * tile, tile), tile)
        pltpu.make_async_copy(gate_ref.at[:, window], gates.at[index], sems.at[2 * index]).wait()
        gate_part = jnp.dot(full_ref[...], gates[index], preferred_element_type=jnp.float32)
        pltpu.make_async_copy(up_ref.at[:, window], ups.at[index], sems.at[2 * index + 1]).wait()
        up_part = jnp.dot(full_ref[...], ups[index], preferred_element_type=jnp.float32)
        act_ref[:, window] = (gate_part / (1.0 + jnp.exp(-gate_part)) * up_part).astype(jnp.bfloat16)
        return carry

    lax.fori_loop(0, tiles, gated, 0)
    copies[2 * tiles].wait()
    copies[2 * tiles + 1].wait()
    given = per_source(out_refs, sources, stride)
    spread = 512

    def lower(index, carry):
        window = pl.ds(pl.multiple_of(index * spread, spread), spread)
        kept = None
        for side in range(2):
            produced = jnp.dot(
                act_ref[...], downs[side, :, window], preferred_element_type=jnp.float32
            )
            rounded = produced[:count].astype(jnp.bfloat16)
            for source, (ref, base) in enumerate(given):
                top = base + side * whole
                ref[top : top + whole, window] = rounded[source * whole : (source + 1) * whole]
            if rest and side == 0:
                kept = produced[count:]
            elif rest:
                moved = pltpu.roll(produced[count:], 4, 0)
                low = lax.broadcasted_iota(jnp.int32, kept.shape, 0) % 8 < 4
                merged = jnp.where(low, kept, moved).astype(jnp.bfloat16)
                for source, (ref, base) in enumerate(given):
                    ref[base + 2 * whole : base + stride, window] = merged[source * 8 : (source + 1) * 8]
        return carry

    lax.fori_loop(0, half // spread, lower, 0)


def run_expert(arrived, weights, sources, whole, rest, arrays_out, tile=256):
    width, units = weights[0].shape
    padded = sources * (whole + (8 if rest else 0))
    stride = 2 * whole + (8 if rest else 0)
    out_shape = jax.ShapeDtypeStruct((sources * stride // arrays_out, width // 2), jnp.bfloat16)
    inside = pl.BlockSpec(memory_space=pltpu.VMEM)
    return pl.pallas_call(
        functools.partial(
            expert_kernel,
            arrays_in=len(arrived),
            arrays_out=arrays_out,
            sources=sources,
            whole=whole,
            rest=rest,
            tile=tile,
        ),
        in_specs=[inside] * len(arrived) + [pl.BlockSpec(memory_space=pl.ANY)] * 3,
        out_specs=[inside] * arrays_out,
        out_shape=[out_shape] * arrays_out,
        scratch_shapes=[
            pltpu.VMEM((padded, width), jnp.bfloat16),
            pltpu.VMEM((padded, units), jnp.bfloat16),
            pltpu.VMEM((units // tile, width, tile), jnp.bfloat16),
            pltpu.VMEM((units // tile, width, tile), jnp.bfloat16),
            pltpu.VMEM((2, units, width // 2), jnp.bfloat16),
            pltpu.SemaphoreType.DMA((2 * (units // tile) + 2,)),
        ],
        compiler_params=pltpu.CompilerParams(vmem_limit_bytes=48 * 1024 * 1024),
        cost_estimate=pl.CostEstimate(
            flops=6 * padded * width * units, transcendentals=padded * units, bytes_accessed=40_000_000
        ),
    )(*arrived, *weights)


def gather_kernel(pick_ref, *refs, block_count):
    block_refs, out_refs = refs[:block_count], refs[block_count:]
    step = pick_ref.shape[0] // len(out_refs)
    spread = 512

    def part(place, carry):
        window = pl.ds(pl.multiple_of(place * spread, spread), spread)
        block = block_refs[0][:, window]
        for ref in block_refs[1:]:
            block = block + ref[:, window]
        for index, ref in enumerate(out_refs):
            ref[:, window] = jnp.dot(
                pick_ref[index * step : (index + 1) * step, :],
                block,
                preferred_element_type=jnp.float32,
            ).astype(jnp.bfloat16)
        return carry

    lax.fori_loop(0, block_refs[0].shape[1] // spread, part, 0)


def gather_rows(pick, blocks, arrays_out):
    out_shape = jax.ShapeDtypeStruct((pick.shape[0] // arrays_out, blocks[0].shape[1]), jnp.bfloat16)
    inside = pl.BlockSpec(memory_space=pltpu.VMEM)
    return pl.pallas_call(
        functools.partial(gather_kernel, block_count=len(blocks)),
        in_specs=[inside] * (1 + len(blocks)),
        out_specs=[inside] * arrays_out,
        out_shape=[out_shape] * arrays_out,
        cost_estimate=pl.CostEstimate(
            flops=2 * pick.size * blocks[0].shape[1], transcendentals=0, bytes_accessed=4_000_000
        ),
    )(pick, *blocks)


def combine_kernel(blend_ref, rows_ref, *out_refs):
    rows = out_refs[0].shape[0]
    spread = 512

    def part(place, carry):
        window = pl.ds(pl.multiple_of(place * spread, spread), spread)
        for index, ref in enumerate(out_refs):
            ref[:, window] = jnp.dot(
                blend_ref[index * rows : (index + 1) * rows, :],
                rows_ref[:, window],
                preferred_element_type=jnp.float32,
            ).astype(ref.dtype)
        return carry

    lax.fori_loop(0, rows_ref.shape[1] // spread, part, 0)


def combine_rows(blend, returned, kind, arrays_out=1):
    out_shape = jax.ShapeDtypeStruct((blend.shape[0] // arrays_out, returned.shape[1]), kind)
    inside = pl.BlockSpec(memory_space=pltpu.VMEM)
    return pl.pallas_call(
        combine_kernel,
        in_specs=[inside] * 2,
        out_specs=[inside] * arrays_out,
        out_shape=[out_shape] * arrays_out,
        cost_estimate=pl.CostEstimate(
            flops=2 * blend.size * out_shape.shape[1], transcendentals=0, bytes_accessed=4_000_000
        ),
    )(blend, returned)


def swap(value, axis, distance, size):
    return lax.ppermute(value, axis, [(i, i ^ distance) for i in range(size)])


def exchange(rows, size):
    if len(rows) > 1:
        return [swap(part, "dp", k, size) if k else part for k, part in enumerate(rows)]
    (rows,) = rows
    parted = rows.reshape(size, rows.shape[0] // size, rows.shape[1])
    parted = lax.all_to_all(parted, "dp", split_axis=0, concat_axis=0, tiled=True)
    return [parted.reshape(rows.shape)]


def after(*values):
    return lax.optimization_barrier(values)


def selection(ids, gates, experts, whole, rest):
    match = (ids[:, :, None] == experts[None, None, :]).astype(jnp.float32)
    chosen = jnp.sum(match, axis=1)
    weight = jnp.sum(match * gates[:, :, None], axis=1)
    rows = ids.shape[0]
    order = jnp.arange(rows, dtype=jnp.int32)
    earlier = (order[:, None] > order[None, :]).astype(jnp.bfloat16)
    ranks = jnp.dot(earlier, chosen.astype(jnp.bfloat16), preferred_element_type=jnp.float32)
    slot_of = jnp.where(chosen > 0, ranks.astype(jnp.int32), -1)
    stride = 2 * whole + (8 if rest else 0)
    column = jnp.arange(experts.shape[0] * stride, dtype=jnp.int32)
    owner, inner = column // stride, column % stride
    ending = inner - 2 * whole
    side = jnp.where(ending < 0, inner // max(whole, 1), ending // 4)
    place = jnp.where(ending < 0, inner % max(whole, 1), whole + ending % 4)
    place = jnp.where(place < whole + rest, place, -2)
    count = column.shape[0]
    expand = owner[None, :] == jnp.arange(experts.shape[0], dtype=jnp.int32)[:, None]
    wide_slot = jnp.sum(jnp.where(expand[None], slot_of[:, :, None], 0), axis=1)
    wide_weight = jnp.sum(jnp.where(expand[None], weight[:, :, None], 0.0), axis=1)
    sides = jnp.arange(2, dtype=jnp.int32)
    hit = (wide_slot == place[None, :])[None] & (side[None, None, :] == sides[:, None, None])
    blend = jnp.where(hit, wide_weight[None], 0.0).reshape(2 * rows, count).astype(jnp.bfloat16)
    pick = hit.reshape(2 * rows, count).astype(jnp.bfloat16).T
    return pick, blend


def per_device(
    residual,
    queries,
    rotated_key_states,
    plain_value_states,
    out_weight,
    norm_gain,
    expert_ids,
    gate_scales,
    w_gate,
    w_up,
    w_down,
):
    row_count = residual.shape[0]
    tensor_size = lax.axis_size("tensor")
    dp_size = lax.axis_size("dp")
    my_tensor = lax.axis_index("tensor")
    my_dp = lax.axis_index("dp")
    heads = QUERY_HEADS // tensor_size
    shares = tensor_size // KEY_VALUE_HEADS

    routing = jnp.concatenate([expert_ids.astype(jnp.float32), gate_scales], axis=1)

    def by_head(states):
        states = states.reshape(row_count, KEY_VALUE_HEADS, HEAD_SIZE)
        return jnp.repeat(states, shares, axis=1) if shares > 1 else states

    slabs = jnp.concatenate(
        [
            queries.reshape(row_count, tensor_size, heads * HEAD_SIZE),
            by_head(rotated_key_states),
            by_head(plain_value_states),
        ],
        axis=2,
    )
    slab = lax.all_to_all(slabs, "tensor", split_axis=1, concat_axis=0, tiled=True)
    slab = slab.reshape(tensor_size * row_count, (heads + 2) * HEAD_SIZE)
    projected = lax.psum_scatter(
        attend_and_project(slab, out_weight, heads),
        "tensor",
        scatter_dimension=0,
        tiled=True,
    ).astype(jnp.float32)
    hidden_state = residual.astype(jnp.float32) + projected
    inverse_rms = lax.rsqrt(jnp.mean(hidden_state * hidden_state, axis=-1, keepdims=True) + 1e-06)
    normed = (hidden_state * inverse_rms * norm_gain.astype(jnp.float32)).astype(jnp.bfloat16)
    normed = jnp.concatenate([normed[:, : D // 2], normed[:, D // 2 :]], axis=0)

    capacity = 9 * row_count // (dp_size * tensor_size)
    peers = jnp.arange(dp_size, dtype=jnp.int32)
    whole, rest = slot_plan(capacity)

    weights = (w_gate[0], w_up[0], w_down[0])

    def plan_for(routing, arrays):
        owners = peers if arrays == 1 else my_dp ^ peers
        return selection(
            routing[:, :TOPK].astype(jnp.int32),
            routing[:, TOPK:],
            owners * tensor_size + my_tensor,
            whole,
            rest,
        )

    def expert(arrived):
        return run_expert(arrived, weights, dp_size, whole, rest, len(arrived))

    def short(value):
        return value.astype(jnp.bfloat16)

    def long(value):
        return value.astype(jnp.float32)

    if tensor_size == 4:
        pairs = [(0, 1), (1, 0), (2, 3), (3, 2)]
        middle = [(1, 2), (2, 1)]
        outward = [(1, 0), (2, 3)]
        inward = [(0, 1), (3, 2)]
        ends = [(0, 3), (3, 0)]
        skips = [(1, 3), (2, 0)]

        def send(value, moves):
            return lax.ppermute(value, "tensor", moves)

        def spread(block):
            near = send(block, pairs)
            inner_two = send(block, middle)
            outer_two = send(inner_two, outward)
            inner_three = send(near, middle)
            outer_three = send(inner_three, outward)
            return near, inner_two, outer_two, inner_three, outer_three

        r_near, r_in2, r_out2, r_in3, r_out3 = spread(routing)
        arrays = (1, 1, 1, 1)
        plans = [
            plan_for(r, n)
            for r, n in zip((routing, r_near, r_in2 + r_out2, r_in3 + r_out3), arrays)
        ]

        normed, *flat = after(normed, *[part for plan in plans for part in plan])
        plans = list(zip(flat[::2], flat[1::2]))

        def dispatch(blocks, chunk):
            return gather_rows(plans[chunk][0], blocks, arrays[chunk])

        def combine(returned, chunk, kind=jnp.bfloat16, arrays_out=1):
            return list(combine_rows(plans[chunk][1], returned[0], kind, arrays_out))

        near = send(normed, pairs)
        inner_two = send(normed, middle)
        out0 = dispatch([normed], 0)
        arr0 = exchange(out0, dp_size)
        near, inner_two, _ = after(near, inner_two, out0)
        outer_two = send(inner_two, outward)
        inner_three = send(near, middle)
        out1 = dispatch([near], 1)
        arr1 = exchange(out1, dp_size)
        arr0, _ = after(arr0, out1)
        pro0 = expert(arr0)
        outer_two, inner_three, _ = after(outer_two, inner_three, pro0)
        outer_three = send(inner_three, outward)
        out2 = dispatch([inner_two, outer_two], 2)
        arr2 = exchange(out2, dp_size)
        arr1, _ = after(arr1, out2)
        pro1 = expert(arr1)
        outer_three, _ = after(outer_three, pro1)
        out3 = dispatch([inner_three, outer_three], 3)
        arr3 = exchange(out3, dp_size)
        arr2, pro1, _ = after(arr2, pro1, out3)
        pro2 = expert(arr2)
        arr3, pro2 = after(arr3, pro2)
        ret2 = exchange(pro2, dp_size)
        pro3 = expert(arr3)
        ret2, pro3 = after(ret2, pro3)
        ret3 = exchange(pro3, dp_size)
        part2 = combine(ret2, 2, arrays_out=2)
        far2 = [send(part2[side], inward) for side in range(2)]
        pro1, ret3, far2[0], far2[1] = after(pro1, ret3, *far2)
        ret1 = exchange(pro1, dp_size)
        part3 = combine(ret3, 3, arrays_out=2)
        far3 = [send(part3[side], inward) for side in range(2)]
        part2[0], part2[1], _ = after(*part2, part3[0])
        last2 = [send(short(long(part2[side]) + long(far2[side])), middle) for side in range(2)]
        pro0, ret1, far3[0], far3[1], last2[0], last2[1] = after(pro0, ret1, *far3, *last2)
        ret0 = exchange(pro0, dp_size)
        mid3 = [send(short(long(part3[0]) + long(far3[0])), middle), None]
        mid3[0], far3[1] = after(mid3[0], far3[1])
        mid3[1] = send(short(long(part3[1]) + long(far3[1])), middle)
        part1 = combine(ret1, 1, jnp.float32, arrays_out=2)
        last1 = [send(short(part1[side] + long(mid3[side])), pairs) for side in range(2)]
        home = combine(ret0, 0, jnp.float32, arrays_out=2)
        moe_sum = jnp.concatenate(
            [home[side] + long(last1[side]) + long(last2[side]) for side in range(2)], axis=0
        )
    else:
        blocks = {0: normed}
        moe_sum = 0.0
        for step in range(tensor_size):
            if step:
                low = step & -step
                blocks[step] = swap(blocks[step ^ low], "tensor", low, tensor_size)
            plan = plan_for(swap(routing, "tensor", step, tensor_size) if step else routing, 1)
            arrived = exchange(gather_rows(plan[0], [blocks[step]], 1), dp_size)
            (blended,) = combine_rows(plan[1], exchange(expert(arrived), dp_size)[0], jnp.float32)
            if step:
                blended = long(swap(short(blended), "tensor", step, tensor_size))
            moe_sum = moe_sum + blended
    moe_sum = jnp.concatenate([moe_sum[:row_count], moe_sum[row_count:]], axis=1)
    return (hidden_state + moe_sum).astype(jnp.bfloat16)


def solution(mesh):
    placed = (
        P(("dp", "tensor"), None),
        P(("dp", "tensor"), None),
        P(("dp", "tensor"), None),
        P(("dp", "tensor"), None),
        P("tensor", None),
        P(),
        P(("dp", "tensor"), None),
        P(("dp", "tensor"), None),
        P(("dp", "tensor"), None, None),
        P(("dp", "tensor"), None, None),
        P(("dp", "tensor"), None, None),
    )
    return jax.shard_map(
        per_device, mesh=mesh, in_specs=placed, out_specs=P(("dp", "tensor"), None), check_vma=False
    )
```

```python
import functools
import math

import jax
import jax.numpy as jnp
from jax import lax
from jax.experimental import pallas as pl
from jax.experimental.pallas import tpu as pltpu
from jax.sharding import PartitionSpec as P

D = 4096
QUERY_HEADS = 32
KEY_VALUE_HEADS = 4
HEAD_SIZE = 128
TOPK = 8


def attend_kernel(
    q_ref, k_ref, v_ref, weight_ref, o_ref, attended_ref, held_ref, sem, *, block, attend_steps
):
    step = pl.program_id(0)
    scaling = 1.0 / math.sqrt(HEAD_SIZE)
    total, lanes = q_ref.shape
    heads = lanes // HEAD_SIZE
    fetch = pltpu.make_async_copy(weight_ref, held_ref, sem)

    @pl.when(step == 0)
    def _():
        fetch.start()

    @pl.when(step < attend_steps)
    def _():
        rows = lax.broadcasted_iota(jnp.int32, (block, block), 0)
        cols = lax.broadcasted_iota(jnp.int32, (block, block), 1)
        for first in range(0, total, block):
            seen = first + block
            mixes = []
            for head in range(heads):
                scores = (
                    lax.dot_general(
                        q_ref[first:seen, head * HEAD_SIZE : (head + 1) * HEAD_SIZE],
                        k_ref[:seen, :],
                        (((1,), (1,)), ((), ())),
                        preferred_element_type=jnp.float32,
                    )
                    * scaling
                )
                diagonal = jnp.where(cols <= rows, scores[:, first:], -1e30)
                if first:
                    scores = jnp.concatenate([scores[:, :first], diagonal], axis=1)
                else:
                    scores = diagonal
                peak = jnp.max(scores, axis=-1, keepdims=True)
                expons = jnp.exp(scores - peak)
                totals = jnp.sum(expons, axis=-1, keepdims=True)
                mixed = jnp.dot(
                    expons.astype(jnp.bfloat16), v_ref[:seen, :], preferred_element_type=jnp.float32
                )
                mixes.append((mixed / totals).astype(jnp.bfloat16))
            start = pl.multiple_of(step * lanes, lanes)
            attended_ref[first:seen, pl.ds(start, lanes)] = jnp.concatenate(mixes, axis=1)

    @pl.when(step == attend_steps)
    def _():
        fetch.wait()

    @pl.when(step >= attend_steps)
    def _():
        tile = o_ref.shape[1]
        start = pl.multiple_of((step - attend_steps) * tile, tile)
        o_ref[...] = jnp.dot(
            attended_ref[...], held_ref[:, pl.ds(start, tile)], preferred_element_type=jnp.float32
        ).astype(jnp.bfloat16)


def attend_and_project(slab, out_weight, heads, tile=512):
    positions = slab.shape[0]
    width = out_weight.shape[1]
    out_weight = pltpu.with_memory_space_constraint(out_weight, pltpu.HBM)
    group = 2 if heads % 2 == 0 else 1
    attend_steps = heads // group
    last = attend_steps - 1
    return pl.pallas_call(
        functools.partial(attend_kernel, block=128, attend_steps=attend_steps),
        grid=(attend_steps + width // tile,),
        in_specs=[
            pl.BlockSpec((positions, group * HEAD_SIZE), lambda i: (0, jnp.minimum(i, last))),
            pl.BlockSpec((positions, HEAD_SIZE), lambda i: (0, heads)),
            pl.BlockSpec((positions, HEAD_SIZE), lambda i: (0, heads + 1)),
            pl.BlockSpec(memory_space=pl.ANY),
        ],
        out_specs=pl.BlockSpec((positions, tile), lambda i: (0, jnp.maximum(i - attend_steps, 0))),
        out_shape=pltpu.HBM((positions, width), jnp.bfloat16),
        scratch_shapes=[
            pltpu.VMEM((positions, heads * HEAD_SIZE), jnp.bfloat16),
            pltpu.VMEM(out_weight.shape, jnp.bfloat16),
            pltpu.SemaphoreType.DMA,
        ],
        compiler_params=pltpu.CompilerParams(vmem_limit_bytes=40 * 1024 * 1024),
    )(slab, slab, slab, out_weight)


def slot_plan(capacity):
    whole = capacity // 8 * 8
    if capacity - whole > 4:
        whole += 8
    return whole, max(capacity - whole, 0)


def per_source(refs, sources, stride):
    if len(refs) == 1:
        return [(refs[0], source * stride) for source in range(sources)]
    return [(ref, 0) for ref in refs]


def expert_kernel(*refs, arrays_in, arrays_out, sources, whole, rest, tile):
    rows_refs, refs = refs[:arrays_in], refs[arrays_in:]
    gate_ref, up_ref, down_ref = refs[:3]
    out_refs, refs = refs[3 : 3 + arrays_out], refs[3 + arrays_out :]
    full_ref, act_ref, gates, ups, downs, sems = refs
    width, units = gate_ref.shape
    half = width // 2
    tiles = units // tile
    pieces = []
    for index in range(tiles):
        window = slice(index * tile, (index + 1) * tile)
        pieces.append((gate_ref.at[:, window], gates.at[index]))
        pieces.append((up_ref.at[:, window], ups.at[index]))
    for side in range(2):
        pieces.append((down_ref.at[:, side * half : (side + 1) * half], downs.at[side]))
    copies = [
        pltpu.make_async_copy(source, target, sems.at[index])
        for index, (source, target) in enumerate(pieces)
    ]
    for copy in copies:
        copy.start()
    stride = 2 * whole + (8 if rest else 0)
    count = sources * whole
    taken = per_source(rows_refs, sources, stride)
    for source, (ref, base) in enumerate(taken):
        for side in range(2):
            first = base + side * whole
            full_ref[source * whole : (source + 1) * whole, side * half : (side + 1) * half] = ref[
                first : first + whole, :
            ]
    if rest:
        last = [ref[base + 2 * whole : base + stride, :].astype(jnp.float32) for ref, base in taken]
        last = jnp.concatenate(last, axis=0)
        full_ref[count:, :half] = last.astype(jnp.bfloat16)
        full_ref[count:, half:] = pltpu.roll(last, last.shape[0] - 4, 0).astype(jnp.bfloat16)
    def gated(index, carry):
        window = pl.ds(pl.multiple_of(index * tile, tile), tile)
        pltpu.make_async_copy(gate_ref.at[:, window], gates.at[index], sems.at[2 * index]).wait()
        gate_part = jnp.dot(full_ref[...], gates[index], preferred_element_type=jnp.float32)
        pltpu.make_async_copy(up_ref.at[:, window], ups.at[index], sems.at[2 * index + 1]).wait()
        up_part = jnp.dot(full_ref[...], ups[index], preferred_element_type=jnp.float32)
        act_ref[:, window] = (gate_part / (1.0 + jnp.exp(-gate_part)) * up_part).astype(jnp.bfloat16)
        return carry

    lax.fori_loop(0, tiles, gated, 0)
    copies[2 * tiles].wait()
    copies[2 * tiles + 1].wait()
    given = per_source(out_refs, sources, stride)
    spread = 512

    def lower(index, carry):
        window = pl.ds(pl.multiple_of(index * spread, spread), spread)
        kept = None
        for side in range(2):
            produced = jnp.dot(
                act_ref[...], downs[side, :, window], preferred_element_type=jnp.float32
            )
            rounded = produced[:count].astype(jnp.bfloat16)
            for source, (ref, base) in enumerate(given):
                top = base + side * whole
                ref[top : top + whole, window] = rounded[source * whole : (source + 1) * whole]
            if rest and side == 0:
                kept = produced[count:]
            elif rest:
                moved = pltpu.roll(produced[count:], 4, 0)
                low = lax.broadcasted_iota(jnp.int32, kept.shape, 0) % 8 < 4
                merged = jnp.where(low, kept, moved).astype(jnp.bfloat16)
                for source, (ref, base) in enumerate(given):
                    ref[base + 2 * whole : base + stride, window] = merged[source * 8 : (source + 1) * 8]
        return carry

    lax.fori_loop(0, half // spread, lower, 0)


def run_expert(arrived, weights, sources, whole, rest, arrays_out, tile=256):
    width, units = weights[0].shape
    padded = sources * (whole + (8 if rest else 0))
    stride = 2 * whole + (8 if rest else 0)
    out_shape = jax.ShapeDtypeStruct((sources * stride // arrays_out, width // 2), jnp.bfloat16)
    inside = pl.BlockSpec(memory_space=pltpu.VMEM)
    return pl.pallas_call(
        functools.partial(
            expert_kernel,
            arrays_in=len(arrived),
            arrays_out=arrays_out,
            sources=sources,
            whole=whole,
            rest=rest,
            tile=tile,
        ),
        in_specs=[inside] * len(arrived) + [pl.BlockSpec(memory_space=pl.ANY)] * 3,
        out_specs=[inside] * arrays_out,
        out_shape=[out_shape] * arrays_out,
        scratch_shapes=[
            pltpu.VMEM((padded, width), jnp.bfloat16),
            pltpu.VMEM((padded, units), jnp.bfloat16),
            pltpu.VMEM((units // tile, width, tile), jnp.bfloat16),
            pltpu.VMEM((units // tile, width, tile), jnp.bfloat16),
            pltpu.VMEM((2, units, width // 2), jnp.bfloat16),
            pltpu.SemaphoreType.DMA((2 * (units // tile) + 2,)),
        ],
        compiler_params=pltpu.CompilerParams(vmem_limit_bytes=48 * 1024 * 1024),
        cost_estimate=pl.CostEstimate(
            flops=6 * padded * width * units, transcendentals=padded * units, bytes_accessed=40_000_000
        ),
    )(*arrived, *weights)


def gather_kernel(pick_ref, *refs, block_count):
    block_refs, out_refs = refs[:block_count], refs[block_count:]
    step = pick_ref.shape[0] // len(out_refs)
    spread = 512

    def part(place, carry):
        window = pl.ds(pl.multiple_of(place * spread, spread), spread)
        block = block_refs[0][:, window]
        for ref in block_refs[1:]:
            block = block + ref[:, window]
        for index, ref in enumerate(out_refs):
            ref[:, window] = jnp.dot(
                pick_ref[index * step : (index + 1) * step, :],
                block,
                preferred_element_type=jnp.float32,
            ).astype(jnp.bfloat16)
        return carry

    lax.fori_loop(0, block_refs[0].shape[1] // spread, part, 0)


def gather_rows(pick, blocks, arrays_out):
    out_shape = jax.ShapeDtypeStruct((pick.shape[0] // arrays_out, blocks[0].shape[1]), jnp.bfloat16)
    inside = pl.BlockSpec(memory_space=pltpu.VMEM)
    return pl.pallas_call(
        functools.partial(gather_kernel, block_count=len(blocks)),
        in_specs=[inside] * (1 + len(blocks)),
        out_specs=[inside] * arrays_out,
        out_shape=[out_shape] * arrays_out,
        cost_estimate=pl.CostEstimate(
            flops=2 * pick.size * blocks[0].shape[1], transcendentals=0, bytes_accessed=4_000_000
        ),
    )(pick, *blocks)


def combine_kernel(blend_ref, rows_ref, *out_refs):
    rows = out_refs[0].shape[0]
    spread = 512

    def part(place, carry):
        window = pl.ds(pl.multiple_of(place * spread, spread), spread)
        for index, ref in enumerate(out_refs):
            ref[:, window] = jnp.dot(
                blend_ref[index * rows : (index + 1) * rows, :],
                rows_ref[:, window],
                preferred_element_type=jnp.float32,
            ).astype(ref.dtype)
        return carry

    lax.fori_loop(0, rows_ref.shape[1] // spread, part, 0)


def combine_rows(blend, returned, kind, arrays_out=1):
    out_shape = jax.ShapeDtypeStruct((blend.shape[0] // arrays_out, returned.shape[1]), kind)
    inside = pl.BlockSpec(memory_space=pltpu.VMEM)
    return pl.pallas_call(
        combine_kernel,
        in_specs=[inside] * 2,
        out_specs=[inside] * arrays_out,
        out_shape=[out_shape] * arrays_out,
        cost_estimate=pl.CostEstimate(
            flops=2 * blend.size * out_shape.shape[1], transcendentals=0, bytes_accessed=4_000_000
        ),
    )(blend, returned)


def swap(value, axis, distance, size):
    return lax.ppermute(value, axis, [(i, i ^ distance) for i in range(size)])


def exchange(rows, size):
    if len(rows) > 1:
        return [swap(part, "dp", k, size) if k else part for k, part in enumerate(rows)]
    (rows,) = rows
    parted = rows.reshape(size, rows.shape[0] // size, rows.shape[1])
    parted = lax.all_to_all(parted, "dp", split_axis=0, concat_axis=0, tiled=True)
    return [parted.reshape(rows.shape)]


def after(*values):
    return lax.optimization_barrier(values)


def selection(ids, gates, experts, whole, rest):
    match = (ids[:, :, None] == experts[None, None, :]).astype(jnp.float32)
    chosen = jnp.sum(match, axis=1)
    weight = jnp.sum(match * gates[:, :, None], axis=1)
    rows = ids.shape[0]
    order = jnp.arange(rows, dtype=jnp.int32)
    earlier = (order[:, None] > order[None, :]).astype(jnp.bfloat16)
    ranks = jnp.dot(earlier, chosen.astype(jnp.bfloat16), preferred_element_type=jnp.float32)
    slot_of = jnp.where(chosen > 0, ranks.astype(jnp.int32), -1)
    stride = 2 * whole + (8 if rest else 0)
    column = jnp.arange(experts.shape[0] * stride, dtype=jnp.int32)
    owner, inner = column // stride, column % stride
    ending = inner - 2 * whole
    side = jnp.where(ending < 0, inner // max(whole, 1), ending // 4)
    place = jnp.where(ending < 0, inner % max(whole, 1), whole + ending % 4)
    place = jnp.where(place < whole + rest, place, -2)
    count = column.shape[0]
    expand = owner[None, :] == jnp.arange(experts.shape[0], dtype=jnp.int32)[:, None]
    wide_slot = jnp.sum(jnp.where(expand[None], slot_of[:, :, None], 0), axis=1)
    wide_weight = jnp.sum(jnp.where(expand[None], weight[:, :, None], 0.0), axis=1)
    sides = jnp.arange(2, dtype=jnp.int32)
    hit = (wide_slot == place[None, :])[None] & (side[None, None, :] == sides[:, None, None])
    blend = jnp.where(hit, wide_weight[None], 0.0).reshape(2 * rows, count).astype(jnp.bfloat16)
    pick = hit.reshape(2 * rows, count).astype(jnp.bfloat16).T
    return pick, blend


def per_device(
    residual,
    queries,
    rotated_key_states,
    plain_value_states,
    out_weight,
    norm_gain,
    expert_ids,
    gate_scales,
    w_gate,
    w_up,
    w_down,
):
    row_count = residual.shape[0]
    tensor_size = lax.axis_size("tensor")
    dp_size = lax.axis_size("dp")
    my_tensor = lax.axis_index("tensor")
    my_dp = lax.axis_index("dp")
    heads = QUERY_HEADS // tensor_size
    shares = tensor_size // KEY_VALUE_HEADS

    routing = jnp.concatenate([expert_ids.astype(jnp.float32), gate_scales], axis=1)

    def by_head(states):
        states = states.reshape(row_count, KEY_VALUE_HEADS, HEAD_SIZE)
        return jnp.repeat(states, shares, axis=1) if shares > 1 else states

    slabs = jnp.concatenate(
        [
            queries.reshape(row_count, tensor_size, heads * HEAD_SIZE),
            by_head(rotated_key_states),
            by_head(plain_value_states),
        ],
        axis=2,
    )
    slab = lax.all_to_all(slabs, "tensor", split_axis=1, concat_axis=0, tiled=True)
    slab = slab.reshape(tensor_size * row_count, (heads + 2) * HEAD_SIZE)
    projected = lax.psum_scatter(
        attend_and_project(slab, out_weight, heads),
        "tensor",
        scatter_dimension=0,
        tiled=True,
    ).astype(jnp.float32)
    hidden_state = residual.astype(jnp.float32) + projected
    inverse_rms = lax.rsqrt(jnp.mean(hidden_state * hidden_state, axis=-1, keepdims=True) + 1e-06)
    normed = (hidden_state * inverse_rms * norm_gain.astype(jnp.float32)).astype(jnp.bfloat16)
    normed = jnp.concatenate([normed[:, : D // 2], normed[:, D // 2 :]], axis=0)

    capacity = 9 * row_count // (dp_size * tensor_size)
    peers = jnp.arange(dp_size, dtype=jnp.int32)
    whole, rest = slot_plan(capacity)

    weights = (w_gate[0], w_up[0], w_down[0])

    def plan_for(routing, arrays):
        owners = peers if arrays == 1 else my_dp ^ peers
        return selection(
            routing[:, :TOPK].astype(jnp.int32),
            routing[:, TOPK:],
            owners * tensor_size + my_tensor,
            whole,
            rest,
        )

    def expert(arrived):
        return run_expert(arrived, weights, dp_size, whole, rest, len(arrived))

    def short(value):
        return value.astype(jnp.bfloat16)

    def long(value):
        return value.astype(jnp.float32)

    if tensor_size == 4:
        pairs = [(0, 1), (1, 0), (2, 3), (3, 2)]
        middle = [(1, 2), (2, 1)]
        outward = [(1, 0), (2, 3)]
        inward = [(0, 1), (3, 2)]
        across = [(0, 2), (3, 1)]

        def send(value, moves):
            return lax.ppermute(value, "tensor", moves)

        def spread(block):
            near = send(block, pairs)
            inner_two = send(block, middle)
            outer_two = send(inner_two, outward)
            inner_three = send(near, middle)
            outer_three = send(inner_three, outward)
            return near, inner_two, outer_two, inner_three, outer_three

        r_near, r_in2, r_out2, r_in3, r_out3 = spread(routing)
        arrays = (1, 1, 1, 1)
        plans = [
            plan_for(r, n)
            for r, n in zip((routing, r_near, r_in2 + r_out2, r_in3 + r_out3), arrays)
        ]

        normed, *flat = after(normed, *[part for plan in plans for part in plan])
        plans = list(zip(flat[::2], flat[1::2]))

        def dispatch(blocks, chunk):
            return gather_rows(plans[chunk][0], blocks, arrays[chunk])

        def combine(returned, chunk, kind=jnp.bfloat16, arrays_out=1):
            return list(combine_rows(plans[chunk][1], returned[0], kind, arrays_out))

        near = send(normed, pairs)
        inner_two = send(normed, middle)
        out0 = dispatch([normed], 0)
        arr0 = exchange(out0, dp_size)
        near, inner_two, _ = after(near, inner_two, out0)
        outer_two = send(inner_two, outward)
        inner_three = send(near, middle)
        out1 = dispatch([near], 1)
        arr1 = exchange(out1, dp_size)
        arr0, _ = after(arr0, out1)
        pro0 = expert(arr0)
        outer_two, inner_three, _ = after(outer_two, inner_three, pro0)
        outer_three = send(inner_three, outward)
        out2 = dispatch([inner_two, outer_two], 2)
        arr2 = exchange(out2, dp_size)
        arr1, _ = after(arr1, out2)
        pro1 = expert(arr1)
        outer_three, _ = after(outer_three, pro1)
        out3 = dispatch([inner_three, outer_three], 3)
        arr3 = exchange(out3, dp_size)
        arr2, pro1, _ = after(arr2, pro1, out3)
        pro2 = expert(arr2)
        arr3, pro2 = after(arr3, pro2)
        ret2 = exchange(pro2, dp_size)
        pro3 = expert(arr3)
        ret2, pro3 = after(ret2, pro3)
        ret3 = exchange(pro3, dp_size)
        (part2,) = combine(ret2, 2)
        outer_back2 = send(part2, across)
        pro1, ret3, outer_back2, part2 = after(pro1, ret3, outer_back2, part2)
        ret1 = exchange(pro1, dp_size)
        part3 = combine(ret3, 3, arrays_out=2)
        far3 = [send(part3[side], inward) for side in range(2)]
        inner_back2 = send(part2, middle)
        inner3 = short(long(part3[0]) + long(far3[0]))
        pro0, ret1, inner3, inner_back2 = after(pro0, ret1, inner3, inner_back2)
        ret0 = exchange(pro0, dp_size)
        mid3 = [send(inner3, middle), None]
        mid3[0], far3[1] = after(mid3[0], far3[1])
        mid3[1] = send(short(long(part3[1]) + long(far3[1])), middle)
        part1 = combine(ret1, 1, jnp.float32, arrays_out=2)
        last1 = [send(short(part1[side] + long(mid3[side])), pairs) for side in range(2)]
        home = combine(ret0, 0, jnp.float32, arrays_out=2)
        back1 = jnp.concatenate([home[side] + long(last1[side]) for side in range(2)], axis=0)
        moe_sum = back1 + long(outer_back2) + long(inner_back2)
    else:
        blocks = {0: normed}
        moe_sum = 0.0
        for step in range(tensor_size):
            if step:
                low = step & -step
                blocks[step] = swap(blocks[step ^ low], "tensor", low, tensor_size)
            plan = plan_for(swap(routing, "tensor", step, tensor_size) if step else routing, 1)
            arrived = exchange(gather_rows(plan[0], [blocks[step]], 1), dp_size)
            (blended,) = combine_rows(plan[1], exchange(expert(arrived), dp_size)[0], jnp.float32)
            if step:
                blended = long(swap(short(blended), "tensor", step, tensor_size))
            moe_sum = moe_sum + blended
    moe_sum = jnp.concatenate([moe_sum[:row_count], moe_sum[row_count:]], axis=1)
    return (hidden_state + moe_sum).astype(jnp.bfloat16)


def solution(mesh):
    placed = (
        P(("dp", "tensor"), None),
        P(("dp", "tensor"), None),
        P(("dp", "tensor"), None),
        P(("dp", "tensor"), None),
        P("tensor", None),
        P(),
        P(("dp", "tensor"), None),
        P(("dp", "tensor"), None),
        P(("dp", "tensor"), None, None),
        P(("dp", "tensor"), None, None),
        P(("dp", "tensor"), None, None),
    )
    return jax.shard_map(
        per_device, mesh=mesh, in_specs=placed, out_specs=P(("dp", "tensor"), None), check_vma=False
    )
```

```python
import functools
import math

import jax
import jax.numpy as jnp
from jax import lax
from jax.experimental import pallas as pl
from jax.experimental.pallas import tpu as pltpu
from jax.sharding import PartitionSpec as P

D = 4096
QUERY_HEADS = 32
KEY_VALUE_HEADS = 4
HEAD_SIZE = 128
TOPK = 8


def attend_kernel(
    q_ref, k_ref, v_ref, weight_ref, o_ref, attended_ref, held_ref, sem, *, block, attend_steps
):
    step = pl.program_id(0)
    scaling = math.log2(math.e) / math.sqrt(HEAD_SIZE)
    total, lanes = q_ref.shape
    heads = lanes // HEAD_SIZE
    fetch = pltpu.make_async_copy(weight_ref, held_ref, sem)

    @pl.when(step == 0)
    def _():
        fetch.start()

    @pl.when(step < attend_steps)
    def _():
        rows = lax.broadcasted_iota(jnp.int32, (block, block), 0)
        cols = lax.broadcasted_iota(jnp.int32, (block, block), 1)
        for first in range(0, total, block):
            seen = first + block
            mixes = []
            for head in range(heads):
                scores = lax.dot_general(
                    q_ref[first:seen, head * HEAD_SIZE : (head + 1) * HEAD_SIZE],
                    k_ref[:seen, :],
                    (((1,), (1,)), ((), ())),
                    preferred_element_type=jnp.float32,
                )
                diagonal = jnp.where(cols <= rows, scores[:, first:], -1e30)
                if first:
                    scores = jnp.concatenate([scores[:, :first], diagonal], axis=1)
                else:
                    scores = diagonal
                peak = jnp.max(scores, axis=-1, keepdims=True)
                expons = jnp.exp2((scores - peak) * scaling)
                totals = jnp.sum(expons, axis=-1, keepdims=True)
                mixed = jnp.dot(
                    expons.astype(jnp.bfloat16), v_ref[:seen, :], preferred_element_type=jnp.float32
                )
                mixes.append((mixed / totals).astype(jnp.bfloat16))
            start = pl.multiple_of(step * lanes, lanes)
            attended_ref[first:seen, pl.ds(start, lanes)] = jnp.concatenate(mixes, axis=1)

    @pl.when(step == attend_steps)
    def _():
        fetch.wait()

    @pl.when(step >= attend_steps)
    def _():
        tile = o_ref.shape[1]
        start = pl.multiple_of((step - attend_steps) * tile, tile)
        o_ref[...] = jnp.dot(
            attended_ref[...], held_ref[:, pl.ds(start, tile)], preferred_element_type=jnp.float32
        ).astype(jnp.bfloat16)


def attend_and_project(slab, out_weight, heads, tile=1024):
    positions = slab.shape[0]
    width = out_weight.shape[1]
    out_weight = pltpu.with_memory_space_constraint(out_weight, pltpu.HBM)
    group = 4 if heads % 4 == 0 else 1
    attend_steps = heads // group
    last = attend_steps - 1
    return pl.pallas_call(
        functools.partial(attend_kernel, block=128, attend_steps=attend_steps),
        grid=(attend_steps + width // tile,),
        in_specs=[
            pl.BlockSpec((positions, group * HEAD_SIZE), lambda i: (0, jnp.minimum(i, last))),
            pl.BlockSpec((positions, HEAD_SIZE), lambda i: (0, heads)),
            pl.BlockSpec((positions, HEAD_SIZE), lambda i: (0, heads + 1)),
            pl.BlockSpec(memory_space=pl.ANY),
        ],
        out_specs=pl.BlockSpec((positions, tile), lambda i: (0, jnp.maximum(i - attend_steps, 0))),
        out_shape=pltpu.HBM((positions, width), jnp.bfloat16),
        scratch_shapes=[
            pltpu.VMEM((positions, heads * HEAD_SIZE), jnp.bfloat16),
            pltpu.VMEM(out_weight.shape, jnp.bfloat16),
            pltpu.SemaphoreType.DMA,
        ],
        compiler_params=pltpu.CompilerParams(vmem_limit_bytes=40 * 1024 * 1024),
    )(slab, slab, slab, out_weight)


def slot_plan(capacity):
    whole = capacity // 8 * 8
    if capacity - whole > 4:
        whole += 8
    return whole, max(capacity - whole, 0)


def per_source(refs, sources, stride):
    if len(refs) == 1:
        return [(refs[0], source * stride) for source in range(sources)]
    return [(ref, 0) for ref in refs]


def expert_kernel(*refs, arrays_in, arrays_out, sources, whole, rest, tile):
    rows_refs, refs = refs[:arrays_in], refs[arrays_in:]
    gate_ref, up_ref, down_ref = refs[:3]
    out_refs, refs = refs[3 : 3 + arrays_out], refs[3 + arrays_out :]
    full_ref, act_ref, gates, ups, downs, sems = refs
    width, units = gate_ref.shape
    half = width // 2
    tiles = units // tile
    pieces = []
    for index in range(tiles):
        window = slice(index * tile, (index + 1) * tile)
        pieces.append((gate_ref.at[:, window], gates.at[index]))
        pieces.append((up_ref.at[:, window], ups.at[index]))
    for side in range(2):
        pieces.append((down_ref.at[:, side * half : (side + 1) * half], downs.at[side]))
    copies = [
        pltpu.make_async_copy(source, target, sems.at[index])
        for index, (source, target) in enumerate(pieces)
    ]
    for copy in copies:
        copy.start()
    stride = 2 * whole + (8 if rest else 0)
    count = sources * whole
    taken = per_source(rows_refs, sources, stride)
    for source, (ref, base) in enumerate(taken):
        for side in range(2):
            first = base + side * whole
            full_ref[source * whole : (source + 1) * whole, side * half : (side + 1) * half] = ref[
                first : first + whole, :
            ]
    if rest:
        last = [ref[base + 2 * whole : base + stride, :].astype(jnp.float32) for ref, base in taken]
        last = jnp.concatenate(last, axis=0)
        full_ref[count:, :half] = last.astype(jnp.bfloat16)
        full_ref[count:, half:] = pltpu.roll(last, last.shape[0] - 4, 0).astype(jnp.bfloat16)
    def gated(index, carry):
        window = pl.ds(pl.multiple_of(index * tile, tile), tile)
        pltpu.make_async_copy(gate_ref.at[:, window], gates.at[index], sems.at[2 * index]).wait()
        gate_part = jnp.dot(full_ref[...], gates[index], preferred_element_type=jnp.float32)
        pltpu.make_async_copy(up_ref.at[:, window], ups.at[index], sems.at[2 * index + 1]).wait()
        up_part = jnp.dot(full_ref[...], ups[index], preferred_element_type=jnp.float32)
        act_ref[:, window] = (gate_part / (1.0 + jnp.exp(-gate_part)) * up_part).astype(jnp.bfloat16)
        return carry

    lax.fori_loop(0, tiles, gated, 0)
    copies[2 * tiles].wait()
    copies[2 * tiles + 1].wait()
    given = per_source(out_refs, sources, stride)
    spread = 512

    def lower(index, carry):
        window = pl.ds(pl.multiple_of(index * spread, spread), spread)
        kept = None
        for side in range(2):
            produced = jnp.dot(
                act_ref[...], downs[side, :, window], preferred_element_type=jnp.float32
            )
            rounded = produced[:count].astype(jnp.bfloat16)
            for source, (ref, base) in enumerate(given):
                top = base + side * whole
                ref[top : top + whole, window] = rounded[source * whole : (source + 1) * whole]
            if rest and side == 0:
                kept = produced[count:]
            elif rest:
                moved = pltpu.roll(produced[count:], 4, 0)
                low = lax.broadcasted_iota(jnp.int32, kept.shape, 0) % 8 < 4
                merged = jnp.where(low, kept, moved).astype(jnp.bfloat16)
                for source, (ref, base) in enumerate(given):
                    ref[base + 2 * whole : base + stride, window] = merged[source * 8 : (source + 1) * 8]
        return carry

    lax.fori_loop(0, half // spread, lower, 0)


def run_expert(arrived, weights, sources, whole, rest, arrays_out, tile=256):
    width, units = weights[0].shape
    padded = sources * (whole + (8 if rest else 0))
    stride = 2 * whole + (8 if rest else 0)
    out_shape = jax.ShapeDtypeStruct((sources * stride // arrays_out, width // 2), jnp.bfloat16)
    inside = pl.BlockSpec(memory_space=pltpu.VMEM)
    return pl.pallas_call(
        functools.partial(
            expert_kernel,
            arrays_in=len(arrived),
            arrays_out=arrays_out,
            sources=sources,
            whole=whole,
            rest=rest,
            tile=tile,
        ),
        in_specs=[inside] * len(arrived) + [pl.BlockSpec(memory_space=pl.ANY)] * 3,
        out_specs=[inside] * arrays_out,
        out_shape=[out_shape] * arrays_out,
        scratch_shapes=[
            pltpu.VMEM((padded, width), jnp.bfloat16),
            pltpu.VMEM((padded, units), jnp.bfloat16),
            pltpu.VMEM((units // tile, width, tile), jnp.bfloat16),
            pltpu.VMEM((units // tile, width, tile), jnp.bfloat16),
            pltpu.VMEM((2, units, width // 2), jnp.bfloat16),
            pltpu.SemaphoreType.DMA((2 * (units // tile) + 2,)),
        ],
        compiler_params=pltpu.CompilerParams(vmem_limit_bytes=48 * 1024 * 1024),
        cost_estimate=pl.CostEstimate(
            flops=6 * padded * width * units, transcendentals=padded * units, bytes_accessed=40_000_000
        ),
    )(*arrived, *weights)


def gather_kernel(pick_ref, *refs, block_count):
    block_refs, out_refs = refs[:block_count], refs[block_count:]
    step = pick_ref.shape[0] // len(out_refs)
    spread = 512

    def part(place, carry):
        window = pl.ds(pl.multiple_of(place * spread, spread), spread)
        block = block_refs[0][:, window]
        for ref in block_refs[1:]:
            block = block + ref[:, window]
        for index, ref in enumerate(out_refs):
            ref[:, window] = jnp.dot(
                pick_ref[index * step : (index + 1) * step, :],
                block,
                preferred_element_type=jnp.float32,
            ).astype(jnp.bfloat16)
        return carry

    lax.fori_loop(0, block_refs[0].shape[1] // spread, part, 0)


def gather_rows(pick, blocks, arrays_out):
    out_shape = jax.ShapeDtypeStruct((pick.shape[0] // arrays_out, blocks[0].shape[1]), jnp.bfloat16)
    inside = pl.BlockSpec(memory_space=pltpu.VMEM)
    return pl.pallas_call(
        functools.partial(gather_kernel, block_count=len(blocks)),
        in_specs=[inside] * (1 + len(blocks)),
        out_specs=[inside] * arrays_out,
        out_shape=[out_shape] * arrays_out,
        cost_estimate=pl.CostEstimate(
            flops=2 * pick.size * blocks[0].shape[1], transcendentals=0, bytes_accessed=4_000_000
        ),
    )(pick, *blocks)


def combine_kernel(blend_ref, rows_ref, *out_refs):
    rows = out_refs[0].shape[0]
    spread = 512

    def part(place, carry):
        window = pl.ds(pl.multiple_of(place * spread, spread), spread)
        for index, ref in enumerate(out_refs):
            ref[:, window] = jnp.dot(
                blend_ref[index * rows : (index + 1) * rows, :],
                rows_ref[:, window],
                preferred_element_type=jnp.float32,
            ).astype(ref.dtype)
        return carry

    lax.fori_loop(0, rows_ref.shape[1] // spread, part, 0)


def combine_rows(blend, returned, kind, arrays_out=1):
    out_shape = jax.ShapeDtypeStruct((blend.shape[0] // arrays_out, returned.shape[1]), kind)
    inside = pl.BlockSpec(memory_space=pltpu.VMEM)
    return pl.pallas_call(
        combine_kernel,
        in_specs=[inside] * 2,
        out_specs=[inside] * arrays_out,
        out_shape=[out_shape] * arrays_out,
        cost_estimate=pl.CostEstimate(
            flops=2 * blend.size * out_shape.shape[1], transcendentals=0, bytes_accessed=4_000_000
        ),
    )(blend, returned)


def swap(value, axis, distance, size):
    return lax.ppermute(value, axis, [(i, i ^ distance) for i in range(size)])


def exchange(rows, size):
    if len(rows) > 1:
        return [swap(part, "dp", k, size) if k else part for k, part in enumerate(rows)]
    (rows,) = rows
    parted = rows.reshape(size, rows.shape[0] // size, rows.shape[1])
    parted = lax.all_to_all(parted, "dp", split_axis=0, concat_axis=0, tiled=True)
    return [parted.reshape(rows.shape)]


def after(*values):
    return lax.optimization_barrier(values)


def selection(ids, gates, experts, whole, rest):
    match = (ids[:, :, None] == experts[None, None, :]).astype(jnp.float32)
    chosen = jnp.sum(match, axis=1)
    weight = jnp.sum(match * gates[:, :, None], axis=1)
    rows = ids.shape[0]
    order = jnp.arange(rows, dtype=jnp.int32)
    earlier = (order[:, None] > order[None, :]).astype(jnp.bfloat16)
    ranks = jnp.dot(earlier, chosen.astype(jnp.bfloat16), preferred_element_type=jnp.float32)
    slot_of = jnp.where(chosen > 0, ranks.astype(jnp.int32), -1)
    stride = 2 * whole + (8 if rest else 0)
    column = jnp.arange(experts.shape[0] * stride, dtype=jnp.int32)
    owner, inner = column // stride, column % stride
    ending = inner - 2 * whole
    side = jnp.where(ending < 0, inner // max(whole, 1), ending // 4)
    place = jnp.where(ending < 0, inner % max(whole, 1), whole + ending % 4)
    place = jnp.where(place < whole + rest, place, -2)
    count = column.shape[0]
    expand = owner[None, :] == jnp.arange(experts.shape[0], dtype=jnp.int32)[:, None]
    wide_slot = jnp.sum(jnp.where(expand[None], slot_of[:, :, None], 0), axis=1)
    wide_weight = jnp.sum(jnp.where(expand[None], weight[:, :, None], 0.0), axis=1)
    sides = jnp.arange(2, dtype=jnp.int32)
    hit = (wide_slot == place[None, :])[None] & (side[None, None, :] == sides[:, None, None])
    blend = jnp.where(hit, wide_weight[None], 0.0).reshape(2 * rows, count).astype(jnp.bfloat16)
    pick = hit.reshape(2 * rows, count).astype(jnp.bfloat16).T
    return pick, blend


def per_device(
    residual,
    queries,
    rotated_key_states,
    plain_value_states,
    out_weight,
    norm_gain,
    expert_ids,
    gate_scales,
    w_gate,
    w_up,
    w_down,
):
    row_count = residual.shape[0]
    tensor_size = lax.axis_size("tensor")
    dp_size = lax.axis_size("dp")
    my_tensor = lax.axis_index("tensor")
    my_dp = lax.axis_index("dp")
    heads = QUERY_HEADS // tensor_size
    shares = tensor_size // KEY_VALUE_HEADS

    routing = jnp.concatenate([expert_ids.astype(jnp.float32), gate_scales], axis=1)

    def by_head(states):
        states = states.reshape(row_count, KEY_VALUE_HEADS, HEAD_SIZE)
        return jnp.repeat(states, shares, axis=1) if shares > 1 else states

    slabs = jnp.concatenate(
        [
            queries.reshape(row_count, tensor_size, heads * HEAD_SIZE),
            by_head(rotated_key_states),
            by_head(plain_value_states),
        ],
        axis=2,
    )
    slab = lax.all_to_all(slabs, "tensor", split_axis=1, concat_axis=0, tiled=True)
    slab = slab.reshape(tensor_size * row_count, (heads + 2) * HEAD_SIZE)
    projected = lax.psum_scatter(
        attend_and_project(slab, out_weight, heads),
        "tensor",
        scatter_dimension=0,
        tiled=True,
    ).astype(jnp.float32)
    hidden_state = residual.astype(jnp.float32) + projected
    inverse_rms = lax.rsqrt(jnp.mean(hidden_state * hidden_state, axis=-1, keepdims=True) + 1e-06)
    normed = (hidden_state * inverse_rms * norm_gain.astype(jnp.float32)).astype(jnp.bfloat16)
    normed = jnp.concatenate([normed[:, : D // 2], normed[:, D // 2 :]], axis=0)

    capacity = 9 * row_count // (dp_size * tensor_size)
    peers = jnp.arange(dp_size, dtype=jnp.int32)
    whole, rest = slot_plan(capacity)

    weights = (w_gate[0], w_up[0], w_down[0])

    def plan_for(routing, arrays):
        owners = peers if arrays == 1 else my_dp ^ peers
        return selection(
            routing[:, :TOPK].astype(jnp.int32),
            routing[:, TOPK:],
            owners * tensor_size + my_tensor,
            whole,
            rest,
        )

    def expert(arrived):
        return run_expert(arrived, weights, dp_size, whole, rest, len(arrived))

    def short(value):
        return value.astype(jnp.bfloat16)

    def long(value):
        return value.astype(jnp.float32)

    if tensor_size == 4:
        pairs = [(0, 1), (1, 0), (2, 3), (3, 2)]
        middle = [(1, 2), (2, 1)]
        outward = [(1, 0), (2, 3)]
        inward = [(0, 1), (3, 2)]
        across = [(0, 2), (3, 1)]

        def send(value, moves):
            return lax.ppermute(value, "tensor", moves)

        def spread(block):
            near = send(block, pairs)
            inner_two = send(block, middle)
            outer_two = send(inner_two, outward)
            inner_three = send(near, middle)
            outer_three = send(inner_three, outward)
            return near, inner_two, outer_two, inner_three, outer_three

        r_near, r_in2, r_out2, r_in3, r_out3 = spread(routing)
        arrays = (1, 1, 1, 1)
        plans = [
            plan_for(r, n)
            for r, n in zip((routing, r_near, r_in2 + r_out2, r_in3 + r_out3), arrays)
        ]

        normed, *flat = after(normed, *[part for plan in plans for part in plan])
        plans = list(zip(flat[::2], flat[1::2]))

        def dispatch(blocks, chunk):
            if len(blocks) == 1:
                pick = plans[chunk][0]
                rows = jnp.dot(pick, blocks[0], preferred_element_type=jnp.float32)
                return [rows.astype(jnp.bfloat16)]
            return gather_rows(plans[chunk][0], blocks, arrays[chunk])

        def combine(returned, chunk, kind=jnp.bfloat16, arrays_out=1):
            return list(combine_rows(plans[chunk][1], returned[0], kind, arrays_out))

        near = send(normed, pairs)
        inner_two = send(normed, middle)
        out0 = dispatch([normed], 0)
        arr0 = exchange(out0, dp_size)
        near, inner_two, _ = after(near, inner_two, out0)
        outer_two = send(inner_two, outward)
        inner_three = send(near, middle)
        out1 = dispatch([near], 1)
        arr1 = exchange(out1, dp_size)
        arr0, _ = after(arr0, out1)
        pro0 = expert(arr0)
        outer_two, inner_three, _ = after(outer_two, inner_three, pro0)
        outer_three = send(inner_three, outward)
        out2 = dispatch([inner_two, outer_two], 2)
        arr2 = exchange(out2, dp_size)
        arr1, _ = after(arr1, out2)
        pro1 = expert(arr1)
        outer_three, _ = after(outer_three, pro1)
        out3 = dispatch([inner_three, outer_three], 3)
        arr3 = exchange(out3, dp_size)
        arr2, pro1, _ = after(arr2, pro1, out3)
        pro2 = expert(arr2)
        arr3, pro2 = after(arr3, pro2)
        ret2 = exchange(pro2, dp_size)
        pro3 = expert(arr3)
        ret2, pro3 = after(ret2, pro3)
        ret3 = exchange(pro3, dp_size)
        (part2,) = combine(ret2, 2)
        outer_back2 = send(part2, across)
        pro1, ret3, outer_back2, part2 = after(pro1, ret3, outer_back2, part2)
        ret1 = exchange(pro1, dp_size)
        part3 = combine(ret3, 3, arrays_out=2)
        far3 = [send(part3[side], inward) for side in range(2)]
        inner_back2 = send(part2, middle)
        inner3 = short(long(part3[0]) + long(far3[0]))
        pro0, ret1, inner3, inner_back2 = after(pro0, ret1, inner3, inner_back2)
        ret0 = exchange(pro0, dp_size)
        mid3 = [send(inner3, middle), None]
        mid3[0], far3[1] = after(mid3[0], far3[1])
        mid3[1] = send(short(long(part3[1]) + long(far3[1])), middle)
        part1 = combine(ret1, 1, jnp.float32, arrays_out=2)
        last1 = [send(short(part1[side] + long(mid3[side])), pairs) for side in range(2)]
        home = combine(ret0, 0, jnp.float32, arrays_out=2)
        back1 = jnp.concatenate([home[side] + long(last1[side]) for side in range(2)], axis=0)
        moe_sum = back1 + long(outer_back2) + long(inner_back2)
    else:
        blocks = {0: normed}
        moe_sum = 0.0
        for step in range(tensor_size):
            if step:
                low = step & -step
                blocks[step] = swap(blocks[step ^ low], "tensor", low, tensor_size)
            plan = plan_for(swap(routing, "tensor", step, tensor_size) if step else routing, 1)
            arrived = exchange(gather_rows(plan[0], [blocks[step]], 1), dp_size)
            (blended,) = combine_rows(plan[1], exchange(expert(arrived), dp_size)[0], jnp.float32)
            if step:
                blended = long(swap(short(blended), "tensor", step, tensor_size))
            moe_sum = moe_sum + blended
    moe_sum = jnp.concatenate([moe_sum[:row_count], moe_sum[row_count:]], axis=1)
    return (hidden_state + moe_sum).astype(jnp.bfloat16)


def solution(mesh):
    placed = (
        P(("dp", "tensor"), None),
        P(("dp", "tensor"), None),
        P(("dp", "tensor"), None),
        P(("dp", "tensor"), None),
        P("tensor", None),
        P(),
        P(("dp", "tensor"), None),
        P(("dp", "tensor"), None),
        P(("dp", "tensor"), None, None),
        P(("dp", "tensor"), None, None),
        P(("dp", "tensor"), None, None),
    )
    return jax.shard_map(
        per_device, mesh=mesh, in_specs=placed, out_specs=P(("dp", "tensor"), None), check_vma=False
    )
```

```python
import functools
import math

import jax
import jax.numpy as jnp
from jax import lax
from jax.experimental import pallas as pl
from jax.experimental.pallas import tpu as pltpu
from jax.sharding import PartitionSpec as P

D = 4096
QUERY_HEADS = 32
KEY_VALUE_HEADS = 4
HEAD_SIZE = 128
TOPK = 8


def attend_kernel(
    q_ref, k_ref, v_ref, weight_ref, o_ref, attended_ref, held_ref, sem, *, block, attend_steps
):
    step = pl.program_id(0)
    scaling = math.log2(math.e) / math.sqrt(HEAD_SIZE)
    total, lanes = q_ref.shape
    heads = lanes // HEAD_SIZE
    fetch = pltpu.make_async_copy(weight_ref, held_ref, sem)

    @pl.when(step == 0)
    def _():
        fetch.start()

    @pl.when(step < attend_steps)
    def _():
        rows = lax.broadcasted_iota(jnp.int32, (block, block), 0)
        cols = lax.broadcasted_iota(jnp.int32, (block, block), 1)
        for first in range(0, total, block):
            seen = first + block
            mixes = []
            for head in range(heads):
                scores = lax.dot_general(
                    q_ref[first:seen, head * HEAD_SIZE : (head + 1) * HEAD_SIZE],
                    k_ref[:seen, :],
                    (((1,), (1,)), ((), ())),
                    preferred_element_type=jnp.float32,
                )
                diagonal = jnp.where(cols <= rows, scores[:, first:], -1e30)
                if first:
                    scores = jnp.concatenate([scores[:, :first], diagonal], axis=1)
                else:
                    scores = diagonal
                peak = jnp.max(scores, axis=-1, keepdims=True)
                expons = jnp.exp2((scores - peak) * scaling)
                totals = jnp.sum(expons, axis=-1, keepdims=True)
                mixed = jnp.dot(
                    expons.astype(jnp.bfloat16), v_ref[:seen, :], preferred_element_type=jnp.float32
                )
                mixes.append((mixed / totals).astype(jnp.bfloat16))
            start = pl.multiple_of(step * lanes, lanes)
            attended_ref[first:seen, pl.ds(start, lanes)] = jnp.concatenate(mixes, axis=1)

    @pl.when(step == attend_steps)
    def _():
        fetch.wait()

    @pl.when(step >= attend_steps)
    def _():
        tile = o_ref.shape[1]
        start = pl.multiple_of((step - attend_steps) * tile, tile)
        o_ref[...] = jnp.dot(
            attended_ref[...], held_ref[:, pl.ds(start, tile)], preferred_element_type=jnp.float32
        ).astype(jnp.bfloat16)


def attend_and_project(slab, out_weight, heads, tile=1024):
    positions = slab.shape[0]
    width = out_weight.shape[1]
    out_weight = pltpu.with_memory_space_constraint(out_weight, pltpu.HBM)
    group = 4 if heads % 4 == 0 else 1
    attend_steps = heads // group
    last = attend_steps - 1
    return pl.pallas_call(
        functools.partial(attend_kernel, block=128, attend_steps=attend_steps),
        grid=(attend_steps + width // tile,),
        in_specs=[
            pl.BlockSpec((positions, group * HEAD_SIZE), lambda i: (0, jnp.minimum(i, last))),
            pl.BlockSpec((positions, HEAD_SIZE), lambda i: (0, heads)),
            pl.BlockSpec((positions, HEAD_SIZE), lambda i: (0, heads + 1)),
            pl.BlockSpec(memory_space=pl.ANY),
        ],
        out_specs=pl.BlockSpec((positions, tile), lambda i: (0, jnp.maximum(i - attend_steps, 0))),
        out_shape=pltpu.HBM((positions, width), jnp.bfloat16),
        scratch_shapes=[
            pltpu.VMEM((positions, heads * HEAD_SIZE), jnp.bfloat16),
            pltpu.VMEM(out_weight.shape, jnp.bfloat16),
            pltpu.SemaphoreType.DMA,
        ],
        compiler_params=pltpu.CompilerParams(vmem_limit_bytes=40 * 1024 * 1024),
    )(slab, slab, slab, out_weight)


def slot_plan(capacity):
    whole = capacity // 8 * 8
    if capacity - whole > 4:
        whole += 8
    return whole, max(capacity - whole, 0)


def per_source(refs, sources, stride):
    if len(refs) == 1:
        return [(refs[0], source * stride) for source in range(sources)]
    return [(ref, 0) for ref in refs]


def expert_kernel(*refs, arrays_in, arrays_out, sources, whole, rest, tile):
    rows_refs, refs = refs[:arrays_in], refs[arrays_in:]
    gate_ref, up_ref, down_ref = refs[:3]
    out_refs, refs = refs[3 : 3 + arrays_out], refs[3 + arrays_out :]
    full_ref, act_ref, gates, ups, downs, sems = refs
    width, units = gate_ref.shape
    half = width // 2
    tiles = units // tile
    pieces = []
    for index in range(tiles):
        window = slice(index * tile, (index + 1) * tile)
        pieces.append((gate_ref.at[:, window], gates.at[index]))
        pieces.append((up_ref.at[:, window], ups.at[index]))
    for side in range(2):
        pieces.append((down_ref.at[:, side * half : (side + 1) * half], downs.at[side]))
    copies = [
        pltpu.make_async_copy(source, target, sems.at[index])
        for index, (source, target) in enumerate(pieces)
    ]
    for copy in copies:
        copy.start()
    stride = 2 * whole + (8 if rest else 0)
    count = sources * whole
    taken = per_source(rows_refs, sources, stride)
    for source, (ref, base) in enumerate(taken):
        for side in range(2):
            first = base + side * whole
            full_ref[source * whole : (source + 1) * whole, side * half : (side + 1) * half] = ref[
                first : first + whole, :
            ]
    if rest:
        last = [ref[base + 2 * whole : base + stride, :].astype(jnp.float32) for ref, base in taken]
        last = jnp.concatenate(last, axis=0)
        full_ref[count:, :half] = last.astype(jnp.bfloat16)
        full_ref[count:, half:] = pltpu.roll(last, last.shape[0] - 4, 0).astype(jnp.bfloat16)
    def gated(index, carry):
        window = pl.ds(pl.multiple_of(index * tile, tile), tile)
        pltpu.make_async_copy(gate_ref.at[:, window], gates.at[index], sems.at[2 * index]).wait()
        gate_part = jnp.dot(full_ref[...], gates[index], preferred_element_type=jnp.float32)
        pltpu.make_async_copy(up_ref.at[:, window], ups.at[index], sems.at[2 * index + 1]).wait()
        up_part = jnp.dot(full_ref[...], ups[index], preferred_element_type=jnp.float32)
        act_ref[:, window] = (gate_part / (1.0 + jnp.exp(-gate_part)) * up_part).astype(jnp.bfloat16)
        return carry

    lax.fori_loop(0, tiles, gated, 0)
    copies[2 * tiles].wait()
    copies[2 * tiles + 1].wait()
    given = per_source(out_refs, sources, stride)
    spread = 512

    def lower(index, carry):
        window = pl.ds(pl.multiple_of(index * spread, spread), spread)
        kept = None
        for side in range(2):
            produced = jnp.dot(
                act_ref[...], downs[side, :, window], preferred_element_type=jnp.float32
            )
            rounded = produced[:count].astype(jnp.bfloat16)
            for source, (ref, base) in enumerate(given):
                top = base + side * whole
                ref[top : top + whole, window] = rounded[source * whole : (source + 1) * whole]
            if rest and side == 0:
                kept = produced[count:]
            elif rest:
                moved = pltpu.roll(produced[count:], 4, 0)
                low = lax.broadcasted_iota(jnp.int32, kept.shape, 0) % 8 < 4
                merged = jnp.where(low, kept, moved).astype(jnp.bfloat16)
                for source, (ref, base) in enumerate(given):
                    ref[base + 2 * whole : base + stride, window] = merged[source * 8 : (source + 1) * 8]
        return carry

    lax.fori_loop(0, half // spread, lower, 0)


def run_expert(arrived, weights, sources, whole, rest, arrays_out, tile=256):
    width, units = weights[0].shape
    padded = sources * (whole + (8 if rest else 0))
    stride = 2 * whole + (8 if rest else 0)
    out_shape = jax.ShapeDtypeStruct((sources * stride // arrays_out, width // 2), jnp.bfloat16)
    inside = pl.BlockSpec(memory_space=pltpu.VMEM)
    return pl.pallas_call(
        functools.partial(
            expert_kernel,
            arrays_in=len(arrived),
            arrays_out=arrays_out,
            sources=sources,
            whole=whole,
            rest=rest,
            tile=tile,
        ),
        in_specs=[inside] * len(arrived) + [pl.BlockSpec(memory_space=pl.ANY)] * 3,
        out_specs=[inside] * arrays_out,
        out_shape=[out_shape] * arrays_out,
        scratch_shapes=[
            pltpu.VMEM((padded, width), jnp.bfloat16),
            pltpu.VMEM((padded, units), jnp.bfloat16),
            pltpu.VMEM((units // tile, width, tile), jnp.bfloat16),
            pltpu.VMEM((units // tile, width, tile), jnp.bfloat16),
            pltpu.VMEM((2, units, width // 2), jnp.bfloat16),
            pltpu.SemaphoreType.DMA((2 * (units // tile) + 2,)),
        ],
        compiler_params=pltpu.CompilerParams(vmem_limit_bytes=48 * 1024 * 1024),
        cost_estimate=pl.CostEstimate(
            flops=6 * padded * width * units, transcendentals=padded * units, bytes_accessed=40_000_000
        ),
    )(*arrived, *weights)


def gather_kernel(pick_ref, *refs, block_count):
    block_refs, out_refs = refs[:block_count], refs[block_count:]
    step = pick_ref.shape[0] // len(out_refs)
    spread = 512

    def part(place, carry):
        window = pl.ds(pl.multiple_of(place * spread, spread), spread)
        block = block_refs[0][:, window]
        for ref in block_refs[1:]:
            block = block + ref[:, window]
        for index, ref in enumerate(out_refs):
            ref[:, window] = jnp.dot(
                pick_ref[index * step : (index + 1) * step, :],
                block,
                preferred_element_type=jnp.float32,
            ).astype(jnp.bfloat16)
        return carry

    lax.fori_loop(0, block_refs[0].shape[1] // spread, part, 0)


def gather_rows(pick, blocks, arrays_out):
    out_shape = jax.ShapeDtypeStruct((pick.shape[0] // arrays_out, blocks[0].shape[1]), jnp.bfloat16)
    inside = pl.BlockSpec(memory_space=pltpu.VMEM)
    return pl.pallas_call(
        functools.partial(gather_kernel, block_count=len(blocks)),
        in_specs=[inside] * (1 + len(blocks)),
        out_specs=[inside] * arrays_out,
        out_shape=[out_shape] * arrays_out,
        cost_estimate=pl.CostEstimate(
            flops=2 * pick.size * blocks[0].shape[1], transcendentals=0, bytes_accessed=4_000_000
        ),
    )(pick, *blocks)


def combine_kernel(blend_ref, rows_ref, *out_refs):
    rows = out_refs[0].shape[0]
    spread = 512

    def part(place, carry):
        window = pl.ds(pl.multiple_of(place * spread, spread), spread)
        for index, ref in enumerate(out_refs):
            ref[:, window] = jnp.dot(
                blend_ref[index * rows : (index + 1) * rows, :],
                rows_ref[:, window],
                preferred_element_type=jnp.float32,
            ).astype(ref.dtype)
        return carry

    lax.fori_loop(0, rows_ref.shape[1] // spread, part, 0)


def combine_rows(blend, returned, kind, arrays_out=1):
    out_shape = jax.ShapeDtypeStruct((blend.shape[0] // arrays_out, returned.shape[1]), kind)
    inside = pl.BlockSpec(memory_space=pltpu.VMEM)
    return pl.pallas_call(
        combine_kernel,
        in_specs=[inside] * 2,
        out_specs=[inside] * arrays_out,
        out_shape=[out_shape] * arrays_out,
        cost_estimate=pl.CostEstimate(
            flops=2 * blend.size * out_shape.shape[1], transcendentals=0, bytes_accessed=4_000_000
        ),
    )(blend, returned)


def swap(value, axis, distance, size):
    return lax.ppermute(value, axis, [(i, i ^ distance) for i in range(size)])


def exchange(rows, size):
    if len(rows) > 1:
        return [swap(part, "dp", k, size) if k else part for k, part in enumerate(rows)]
    (rows,) = rows
    parted = rows.reshape(size, rows.shape[0] // size, rows.shape[1])
    parted = lax.all_to_all(parted, "dp", split_axis=0, concat_axis=0, tiled=True)
    return [parted.reshape(rows.shape)]


def after(*values):
    return lax.optimization_barrier(values)


def selection(ids, gates, experts, whole, rest):
    match = (ids[:, :, None] == experts[None, None, :]).astype(jnp.float32)
    chosen = jnp.sum(match, axis=1)
    weight = jnp.sum(match * gates[:, :, None], axis=1)
    rows = ids.shape[0]
    order = jnp.arange(rows, dtype=jnp.int32)
    earlier = (order[:, None] > order[None, :]).astype(jnp.bfloat16)
    ranks = jnp.dot(earlier, chosen.astype(jnp.bfloat16), preferred_element_type=jnp.float32)
    slot_of = jnp.where(chosen > 0, ranks.astype(jnp.int32), -1)
    stride = 2 * whole + (8 if rest else 0)
    column = jnp.arange(experts.shape[0] * stride, dtype=jnp.int32)
    owner, inner = column // stride, column % stride
    ending = inner - 2 * whole
    side = jnp.where(ending < 0, inner // max(whole, 1), ending // 4)
    place = jnp.where(ending < 0, inner % max(whole, 1), whole + ending % 4)
    place = jnp.where(place < whole + rest, place, -2)
    count = column.shape[0]
    expand = owner[None, :] == jnp.arange(experts.shape[0], dtype=jnp.int32)[:, None]
    wide_slot = jnp.sum(jnp.where(expand[None], slot_of[:, :, None], 0), axis=1)
    wide_weight = jnp.sum(jnp.where(expand[None], weight[:, :, None], 0.0), axis=1)
    sides = jnp.arange(2, dtype=jnp.int32)
    hit = (wide_slot == place[None, :])[None] & (side[None, None, :] == sides[:, None, None])
    blend = jnp.where(hit, wide_weight[None], 0.0).reshape(2 * rows, count).astype(jnp.bfloat16)
    pick = hit.reshape(2 * rows, count).astype(jnp.bfloat16).T
    return pick, blend


def per_device(
    residual,
    queries,
    rotated_key_states,
    plain_value_states,
    out_weight,
    norm_gain,
    expert_ids,
    gate_scales,
    w_gate,
    w_up,
    w_down,
):
    row_count = residual.shape[0]
    tensor_size = lax.axis_size("tensor")
    dp_size = lax.axis_size("dp")
    my_tensor = lax.axis_index("tensor")
    my_dp = lax.axis_index("dp")
    heads = QUERY_HEADS // tensor_size
    shares = tensor_size // KEY_VALUE_HEADS

    routing = jnp.concatenate([expert_ids.astype(jnp.float32), gate_scales], axis=1)

    def by_head(states):
        states = states.reshape(row_count, KEY_VALUE_HEADS, HEAD_SIZE)
        return jnp.repeat(states, shares, axis=1) if shares > 1 else states

    slabs = jnp.concatenate(
        [
            queries.reshape(row_count, tensor_size, heads * HEAD_SIZE),
            by_head(rotated_key_states),
            by_head(plain_value_states),
        ],
        axis=2,
    )
    slab = lax.all_to_all(slabs, "tensor", split_axis=1, concat_axis=0, tiled=True)
    slab = slab.reshape(tensor_size * row_count, (heads + 2) * HEAD_SIZE)
    projected = lax.psum_scatter(
        attend_and_project(slab, out_weight, heads),
        "tensor",
        scatter_dimension=0,
        tiled=True,
    ).astype(jnp.float32)
    hidden_state = residual.astype(jnp.float32) + projected
    inverse_rms = lax.rsqrt(jnp.mean(hidden_state * hidden_state, axis=-1, keepdims=True) + 1e-06)
    normed = (hidden_state * inverse_rms * norm_gain.astype(jnp.float32)).astype(jnp.bfloat16)
    normed = jnp.concatenate([normed[:, : D // 2], normed[:, D // 2 :]], axis=0)

    capacity = 9 * row_count // (dp_size * tensor_size)
    peers = jnp.arange(dp_size, dtype=jnp.int32)
    whole, rest = slot_plan(capacity)

    weights = (w_gate[0], w_up[0], w_down[0])

    def plan_for(routing, arrays):
        owners = peers if arrays == 1 else my_dp ^ peers
        return selection(
            routing[:, :TOPK].astype(jnp.int32),
            routing[:, TOPK:],
            owners * tensor_size + my_tensor,
            whole,
            rest,
        )

    def expert(arrived):
        return run_expert(arrived, weights, dp_size, whole, rest, len(arrived))

    def short(value):
        return value.astype(jnp.bfloat16)

    def long(value):
        return value.astype(jnp.float32)

    if tensor_size == 4:
        pairs = [(0, 1), (1, 0), (2, 3), (3, 2)]
        middle = [(1, 2), (2, 1)]
        outward = [(1, 0), (2, 3)]
        inward = [(0, 1), (3, 2)]
        across = [(0, 2), (3, 1)]

        def send(value, moves):
            return lax.ppermute(value, "tensor", moves)

        def spread(block):
            near = send(block, pairs)
            inner_two = send(block, middle)
            outer_two = send(inner_two, outward)
            inner_three = send(near, middle)
            outer_three = send(inner_three, outward)
            return near, inner_two, outer_two, inner_three, outer_three

        r_near, r_in2, r_out2, r_in3, r_out3 = spread(routing)
        arrays = (1, 1, 1, 1)
        plans = [
            plan_for(r, n)
            for r, n in zip((routing, r_near, r_in2 + r_out2, r_in3 + r_out3), arrays)
        ]

        normed, *flat = after(normed, *[part for plan in plans for part in plan])
        plans = list(zip(flat[::2], flat[1::2]))

        def dispatch(blocks, chunk):
            if len(blocks) == 1:
                pick = plans[chunk][0]
                rows = jnp.dot(pick, blocks[0], preferred_element_type=jnp.float32)
                return [rows.astype(jnp.bfloat16)]
            return gather_rows(plans[chunk][0], blocks, arrays[chunk])

        def combine(returned, chunk, kind=jnp.bfloat16, arrays_out=1):
            return list(combine_rows(plans[chunk][1], returned[0], kind, arrays_out))

        near = send(normed, pairs)
        inner_two = send(normed, middle)
        out0 = dispatch([normed], 0)
        arr0 = exchange(out0, dp_size)
        near, inner_two, _ = after(near, inner_two, out0)
        outer_two = send(inner_two, outward)
        inner_three = send(near, middle)
        out1 = dispatch([near], 1)
        arr1 = exchange(out1, dp_size)
        arr0, _ = after(arr0, out1)
        pro0 = expert(arr0)
        outer_two, inner_three, _ = after(outer_two, inner_three, pro0)
        outer_three = send(inner_three, outward)
        out2 = dispatch([inner_two, outer_two], 2)
        arr2 = exchange(out2, dp_size)
        arr1, _ = after(arr1, out2)
        pro1 = expert(arr1)
        outer_three, _ = after(outer_three, pro1)
        out3 = dispatch([inner_three, outer_three], 3)
        arr3 = exchange(out3, dp_size)
        arr2, pro1, _ = after(arr2, pro1, out3)
        pro2 = expert(arr2)
        arr3, pro2 = after(arr3, pro2)
        ret2 = exchange(pro2, dp_size)
        pro3 = expert(arr3)
        ret2, pro3 = after(ret2, pro3)
        ret3 = exchange(pro3, dp_size)
        (part2,) = combine(ret2, 2)
        outer_back2 = send(part2, across)
        pro1, ret3, outer_back2, part2 = after(pro1, ret3, outer_back2, part2)
        ret1 = exchange(pro1, dp_size)
        blend3 = plans[3][1]
        part3 = list(combine_rows(blend3[:row_count], ret3[0], jnp.bfloat16))
        far3 = [send(part3[0], inward), None]
        ret3[0], _ = after(ret3[0], part3[0])
        part3 += combine_rows(blend3[row_count:], ret3[0], jnp.bfloat16)
        far3[1] = send(part3[1], inward)
        inner_back2 = send(part2, middle)
        inner3 = short(long(part3[0]) + long(far3[0]))
        pro0, ret1, inner3, inner_back2 = after(pro0, ret1, inner3, inner_back2)
        ret0 = exchange(pro0, dp_size)
        mid3 = [send(inner3, middle), None]
        mid3[0], far3[1] = after(mid3[0], far3[1])
        mid3[1] = send(short(long(part3[1]) + long(far3[1])), middle)
        part1 = combine(ret1, 1, jnp.float32, arrays_out=2)
        last1 = [send(short(part1[side] + long(mid3[side])), pairs) for side in range(2)]
        home = combine(ret0, 0, jnp.float32, arrays_out=2)
        back1 = jnp.concatenate([home[side] + long(last1[side]) for side in range(2)], axis=0)
        moe_sum = back1 + long(outer_back2) + long(inner_back2)
    else:
        blocks = {0: normed}
        moe_sum = 0.0
        for step in range(tensor_size):
            if step:
                low = step & -step
                blocks[step] = swap(blocks[step ^ low], "tensor", low, tensor_size)
            plan = plan_for(swap(routing, "tensor", step, tensor_size) if step else routing, 1)
            arrived = exchange(gather_rows(plan[0], [blocks[step]], 1), dp_size)
            (blended,) = combine_rows(plan[1], exchange(expert(arrived), dp_size)[0], jnp.float32)
            if step:
                blended = long(swap(short(blended), "tensor", step, tensor_size))
            moe_sum = moe_sum + blended
    moe_sum = jnp.concatenate([moe_sum[:row_count], moe_sum[row_count:]], axis=1)
    return (hidden_state + moe_sum).astype(jnp.bfloat16)


def solution(mesh):
    placed = (
        P(("dp", "tensor"), None),
        P(("dp", "tensor"), None),
        P(("dp", "tensor"), None),
        P(("dp", "tensor"), None),
        P("tensor", None),
        P(),
        P(("dp", "tensor"), None),
        P(("dp", "tensor"), None),
        P(("dp", "tensor"), None, None),
        P(("dp", "tensor"), None, None),
        P(("dp", "tensor"), None, None),
    )
    return jax.shard_map(
        per_device, mesh=mesh, in_specs=placed, out_specs=P(("dp", "tensor"), None), check_vma=False
    )
```
